32 devices in a mesh: seq: 8 (over z, y), head: 4 (over x, core).
Axes of the slice: x: 2, y: 2, z: 4, core: 2. Of those that a mesh axis runs over, the one named last changes fastest.
Arguments:
- queries: bfloat16 [1024, 8, 128], P('seq', 'head'), may hold values from -16 to 16
- values: bfloat16 [1024, 8, 128], P('seq', 'head'), may hold values from -6 to 6
- codes: int32 [8, 1024], P('head', 'seq'), may hold values from 0 to 511, as said below
- codebook: bfloat16 [8, 512, 128], P('head'), may hold values from -0.5 to 0.5
- out_weight: bfloat16 [1024, 2048], P('head'), may hold values from -0.1875 to 0.1875
- grad_out: bfloat16 [1024, 2048], P('seq', 'head'), may hold values from -6 to 6
Outputs:
- grad_queries: bfloat16 [1024, 8, 128], P('seq', 'head')
- grad_values: bfloat16 [1024, 8, 128], P('seq', 'head')
- grad_codebook: float32 [8, 512, 128], P('head')
- grad_weight: bfloat16 [1024, 2048], P('head')
The draws below stay inside these ranges and needn't reach their ends.
Inputs may be any that keep to these rules, and one draw needn't show every extreme that they name: `codes`: each head's key codeword at each token; both 0 and 511 occur.
All inputs are finite; a program needn't handle non-finite values.
Results may differ from the reference program's by a relative error of at most 0.0065.
Values may be sent and summed in bfloat16 or wider, within the bound.
No kernel may reach another device: no remote copies, remote signals or barrier semaphores. Data moves between devices by JAX's collectives and lax.ppermute only.
A program may use at most 256 MiB of HBM per device.

```python
import math
import jax
import jax.numpy as jnp
from jax import lax

D = 2048
HEADS = 8
HEAD_DIM = 128
CODES = 512
BLOCK = 128
TOKENS = 1024


def codebook_values(key):
    book_key = jax.random.fold_in(key, 7)
    return 0.09 * jax.random.truncated_normal(book_key, -4.0, 4.0, (HEADS, CODES, HEAD_DIM), jnp.float32)


def code_table(key):
    code_rows = jax.random.randint(jax.random.fold_in(key, 13), (HEADS, TOKENS), 0, CODES, dtype=jnp.int32)
    code_rows = code_rows.at[:, 0].set(CODES - 1)
    return code_rows.at[:, 1].set(0)


def draw_codes(key, part):
    return code_table(key)


def draw_codebook(key, part):
    return codebook_values(key).astype(jnp.bfloat16)


def draw_queries(key, part):
    full_shape = (TOKENS, HEADS, HEAD_DIM)
    row_scale = jnp.exp(jax.random.uniform(jax.random.fold_in(key, 21), (TOKENS, HEADS, 1), jnp.float32, math.log(0.3), math.log(3.0)))
    return (jax.random.truncated_normal(jax.random.fold_in(key, 22), -4.0, 4.0, full_shape, jnp.float32) * row_scale).astype(jnp.bfloat16)


def block_scale(key, shape, shards, low, top_value):
    level = 1.0
    for axis_at, shards_of in shards:
        draws = jax.random.uniform(jax.random.fold_in(jax.random.fold_in(key, 6), axis_at), (shards_of,), jnp.float32, low / len(shards), top_value / len(shards))
        level = level * jnp.repeat(jnp.exp(draws), shape[axis_at] // shards_of).reshape((-1,) + (1,) * (len(shape) - 1 - axis_at))
    return level


def gaussian(stream_key, shape, spread, limit, cuts=(), held_as=jnp.bfloat16):
    level = block_scale(stream_key, shape, cuts, -0.22, 0.18) if cuts else 1.0
    entries = jax.random.normal(stream_key, shape, jnp.float32) * spread * level
    return jnp.minimum(jnp.maximum(entries, -limit), limit).astype(held_as)


def setup_inputs(seed: int = 0) -> dict:
    splits = jax.random.split(jax.random.key(seed), 7)
    return {
        "queries": draw_queries(jax.random.fold_in(splits[6], 71), 0),
        "values": gaussian(splits[1], (TOKENS, HEADS, HEAD_DIM), 1.0, 6.0, ((0, 8), (1, 4))),
        "codes": draw_codes(jax.random.fold_in(splits[6], 71), 0),
        "codebook": draw_codebook(jax.random.fold_in(splits[6], 71), 0),
        "out_weight": gaussian(splits[4], (HEADS * HEAD_DIM, D), (HEADS * HEAD_DIM) ** -0.5, 0.1875, ((0, 4),)),
        "grad_out": gaussian(splits[5], (TOKENS, D), 1.0, 6.0, ((0, 8), (1, 4))),
    }


def block_core(query_rows, code_rows, value_rows, grad_rows, cache_sum, cache_count, codebook_head):
    key_rows = jnp.take(codebook_head, code_rows, axis=0)
    local_score = jnp.dot(query_rows, key_rows.T, preferred_element_type=jnp.float32)
    code_score = jnp.dot(query_rows, codebook_head.T, preferred_element_type=jnp.float32)
    length = query_rows.shape[0]
    row_index = lax.broadcasted_iota(jnp.int32, (length, length), 0)
    col_index = lax.broadcasted_iota(jnp.int32, (length, length), 1)
    causal = col_index <= row_index
    top_score = jnp.maximum(jnp.max(jnp.where(causal, local_score, -jnp.inf), axis=1), jnp.max(code_score, axis=1))
    weights = jnp.where(causal, jnp.exp(local_score - top_score[:, None]), jnp.float32(0.0))
    cache_weight = jnp.exp(code_score - top_score[:, None])
    denominator = jnp.sum(weights, axis=1) + jnp.sum(cache_weight * cache_count[None, :], axis=1)
    cache_round = cache_sum.astype(jnp.bfloat16)
    numerator = jnp.dot(weights.astype(jnp.bfloat16), value_rows, preferred_element_type=jnp.float32)
    numerator = numerator + jnp.dot(cache_weight.astype(jnp.bfloat16), cache_round, preferred_element_type=jnp.float32)
    attended = numerator / denominator[:, None]
    row_delta = jnp.sum(grad_rows.astype(jnp.float32) * attended, axis=1)
    local_grad = jnp.dot(grad_rows, value_rows.T, preferred_element_type=jnp.float32)
    cache_grad = jnp.dot(grad_rows, cache_round.T, preferred_element_type=jnp.float32)
    grad_local = (weights * (local_grad - row_delta[:, None]) / denominator[:, None]).astype(jnp.bfloat16)
    grad_cache = (cache_weight * (cache_grad - row_delta[:, None] * cache_count[None, :]) / denominator[:, None]).astype(jnp.bfloat16)
    grad_query = jnp.dot(grad_local, key_rows, preferred_element_type=jnp.float32)
    grad_query = (grad_query + jnp.dot(grad_cache, codebook_head, preferred_element_type=jnp.float32)).astype(jnp.bfloat16)
    grad_key = jnp.dot(grad_local.T, query_rows, preferred_element_type=jnp.float32)
    grad_book = jax.ops.segment_sum(grad_key, code_rows, num_segments=codebook_head.shape[0])
    grad_book = grad_book + jnp.dot(grad_cache.T, query_rows, preferred_element_type=jnp.float32)
    local_share = (weights / denominator[:, None]).astype(jnp.bfloat16)
    cache_share = (cache_weight / denominator[:, None]).astype(jnp.bfloat16)
    grad_value = jnp.dot(local_share.T, grad_rows, preferred_element_type=jnp.float32)
    grad_sum = jnp.dot(cache_share.T, grad_rows, preferred_element_type=jnp.float32)
    return grad_query, grad_value, grad_sum, grad_book, attended.astype(jnp.bfloat16)


def reference(queries, values, codes, codebook, out_weight, grad_out):
    blocks = TOKENS // BLOCK

    def one_head(items):
        weight_head, query_head, value_head, code_head, codebook_head = items
        grad_head = jnp.dot(grad_out, weight_head.T, preferred_element_type=jnp.float32).astype(jnp.bfloat16)
        query_blocks = query_head.reshape(blocks, BLOCK, HEAD_DIM)
        value_blocks = value_head.reshape(blocks, BLOCK, HEAD_DIM)
        grad_blocks = grad_head.reshape(blocks, BLOCK, HEAD_DIM)
        code_blocks = code_head.reshape(blocks, BLOCK)

        def forward(carry, block_items):
            cache_sum, cache_count, book_total = carry
            query_rows, code_rows, value_rows, grad_rows = block_items
            grad_query, grad_value, grad_sum, grad_book, attended = block_core(
                query_rows, code_rows, value_rows, grad_rows, cache_sum, cache_count, codebook_head)
            cache_sum = cache_sum + jax.ops.segment_sum(value_rows.astype(jnp.float32), code_rows, num_segments=CODES)
            cache_count = cache_count + jax.ops.segment_sum(jnp.ones((BLOCK,), jnp.float32), code_rows, num_segments=CODES)
            return (cache_sum, cache_count, book_total + grad_book), (grad_query, grad_value, grad_sum, attended)

        start = (jnp.zeros((CODES, HEAD_DIM), jnp.float32), jnp.zeros((CODES,), jnp.float32), jnp.zeros((CODES, HEAD_DIM), jnp.float32))
        final, stacked = lax.scan(forward, start, (query_blocks, code_blocks, value_blocks, grad_blocks))
        book_total = final[2]
        grad_query, grad_value, grad_sums, attended = stacked

        def backward(carry, block_items):
            grad_sum, grad_value_rows, code_rows = block_items
            finished = (grad_value_rows + jnp.take(carry, code_rows, axis=0)).astype(jnp.bfloat16)
            return carry + grad_sum, finished

        unused, grad_values_head = lax.scan(backward, jnp.zeros((CODES, HEAD_DIM), jnp.float32), (grad_sums, grad_value, code_blocks), reverse=True)
        weight_grad = jnp.dot(attended.reshape(TOKENS, HEAD_DIM).T, grad_out, preferred_element_type=jnp.float32).astype(jnp.bfloat16)
        return grad_query.reshape(TOKENS, HEAD_DIM), grad_values_head.reshape(TOKENS, HEAD_DIM), book_total, weight_grad

    results = lax.map(one_head, (out_weight.reshape(HEADS, HEAD_DIM, D), jnp.moveaxis(queries, 1, 0), jnp.moveaxis(values, 1, 0), codes, codebook))
    grad_queries = jnp.moveaxis(results[0], 0, 1)
    grad_values = jnp.moveaxis(results[1], 0, 1)
    return grad_queries, grad_values, results[2], results[3].reshape(HEADS * HEAD_DIM, D)
```

```python
import functools

import jax
import jax.numpy as jnp
from jax import lax
from jax.experimental import pallas as pl
from jax.experimental.pallas import tpu as pltpu
from jax.sharding import PartitionSpec as P

BLOCK = 128


def entering(value, axis, join, neutral, backward):
    count, mine = (lax.axis_size(axis), lax.axis_index(axis))
    pieces = jax.tree.map(lambda part: lax.all_gather(part, axis), value)
    if backward:
        pieces = jax.tree.map(lambda part: part[::-1], pieces)
        mine = count - 1 - mine
    so_far = jax.tree.map(
        lambda part, zero: jnp.full_like(part, 0) + jnp.asarray(zero, part.dtype), value, neutral
    )

    def turn(position, so_far):
        longer = join(so_far, jax.tree.map(lambda part: part[position], pieces))
        return jax.tree.map(lambda new, old: jnp.where(position < mine, new, old), longer, so_far)

    return lax.fori_loop(0, count - 1, turn, so_far)


def inner_rows(left_side, right_side):
    return lax.dot_general(
        left_side, right_side, (((0,), (0,)), ((), ())), preferred_element_type=jnp.float32
    )


def block_core(query_rows, code_rows, value_rows, grad_rows, cache_sum, cache_count, codebook_head):
    key_rows = jnp.take(codebook_head, code_rows, axis=0)
    contract_last = (((1,), (1,)), ((), ()))
    local_score = lax.dot_general(
        query_rows, key_rows, contract_last, preferred_element_type=jnp.float32
    )
    code_score = lax.dot_general(
        query_rows, codebook_head, contract_last, preferred_element_type=jnp.float32
    )
    length = query_rows.shape[0]
    row_index = lax.broadcasted_iota(jnp.int32, (length, length), 0)
    col_index = lax.broadcasted_iota(jnp.int32, (length, length), 1)
    causal = col_index <= row_index
    top_score = jnp.maximum(
        jnp.max(jnp.where(causal, local_score, -jnp.inf), axis=1), jnp.max(code_score, axis=1)
    )
    weights = jnp.where(causal, jnp.exp(local_score - top_score[:, None]), jnp.float32(0.0))
    cache_weight = jnp.exp(code_score - top_score[:, None])
    denominator = jnp.sum(weights, axis=1) + jnp.sum(cache_weight * cache_count[None, :], axis=1)
    cache_round = cache_sum.astype(jnp.bfloat16)
    numerator = jnp.dot(
        weights.astype(jnp.bfloat16), value_rows, preferred_element_type=jnp.float32
    )
    numerator = numerator + jnp.dot(
        cache_weight.astype(jnp.bfloat16), cache_round, preferred_element_type=jnp.float32
    )
    attended = numerator / denominator[:, None]
    row_delta = jnp.sum(grad_rows.astype(jnp.float32) * attended, axis=1)
    local_grad = lax.dot_general(
        grad_rows, value_rows, contract_last, preferred_element_type=jnp.float32
    )
    cache_grad = lax.dot_general(
        grad_rows, cache_round, contract_last, preferred_element_type=jnp.float32
    )
    grad_local = (weights * (local_grad - row_delta[:, None]) / denominator[:, None]).astype(
        jnp.bfloat16
    )
    grad_cache = (
        cache_weight
        * (cache_grad - row_delta[:, None] * cache_count[None, :])
        / denominator[:, None]
    ).astype(jnp.bfloat16)
    grad_query = jnp.dot(grad_local, key_rows, preferred_element_type=jnp.float32)
    grad_query = (
        grad_query + jnp.dot(grad_cache, codebook_head, preferred_element_type=jnp.float32)
    ).astype(jnp.bfloat16)
    grad_key = inner_rows(grad_local, query_rows)
    key_high = grad_key.astype(jnp.bfloat16)
    key_low = (grad_key - key_high.astype(jnp.float32)).astype(jnp.bfloat16)
    selector = (
        code_rows[:, None] == jnp.arange(codebook_head.shape[0], dtype=jnp.int32)[None, :]
    ).astype(jnp.bfloat16)
    grad_book = inner_rows(selector, key_high) + inner_rows(selector, key_low)
    grad_book = grad_book + inner_rows(grad_cache, query_rows)
    local_share = (weights / denominator[:, None]).astype(jnp.bfloat16)
    cache_share = (cache_weight / denominator[:, None]).astype(jnp.bfloat16)
    grad_value = inner_rows(local_share, grad_rows)
    grad_sum = inner_rows(cache_share, grad_rows)
    return (grad_query, grad_value, grad_sum, grad_book, attended.astype(jnp.bfloat16))


def exclusive_forward(stacked):
    summed = jnp.cumsum(stacked, axis=1)
    return jnp.concatenate([jnp.zeros_like(stacked), summed[:, :-1]], axis=1)


def exclusive_backward(stacked):
    summed = jnp.flip(jnp.cumsum(jnp.flip(stacked, axis=1), axis=1), axis=1)
    return jnp.concatenate([summed[:, 1:], jnp.zeros_like(stacked)], axis=1)


def on_device(queries, values, codes, codebook, out_weight, grad_out):
    tok_here, heads_here, head_width = queries.shape
    code_total = codebook.shape[1]
    blocks = tok_here // BLOCK
    full_grad = lax.all_gather(grad_out, "head", axis=1, tiled=True)
    grad_flat = lax.dot_general(
        full_grad, out_weight, (((1,), (1,)), ((), ())), preferred_element_type=jnp.float32
    ).astype(jnp.bfloat16)
    grad_heads = grad_flat.reshape(tok_here, heads_here, head_width)

    def to_blocks(array):
        return jnp.moveaxis(array.reshape(blocks, BLOCK, heads_here, head_width), 2, 0)

    def from_blocks(array):
        return jnp.moveaxis(array, 0, 2).reshape(tok_here, heads_here, head_width)

    def flatten(array):
        return array.reshape((heads_here * blocks,) + array.shape[2:])

    def unflatten(array):
        return array.reshape((heads_here, blocks) + array.shape[1:])

    code_blocks = codes.reshape(heads_here, blocks, BLOCK)
    query_blocks = to_blocks(queries)
    value_blocks = to_blocks(values)
    grad_blocks = to_blocks(grad_heads)
    selector = (code_blocks[..., None] == jnp.arange(code_total, dtype=jnp.int32)).astype(
        jnp.bfloat16
    )
    block_sums = jnp.einsum(
        "hnbc,hnbd->hncd", selector, value_blocks, preferred_element_type=jnp.float32
    )
    block_counts = jnp.sum(selector, axis=2, dtype=jnp.float32)
    device_parts = (jnp.sum(block_sums, axis=1), jnp.sum(block_counts, axis=1))
    earlier = entering(
        device_parts,
        "seq",
        lambda first_part, second_part: (
            first_part[0] + second_part[0],
            first_part[1] + second_part[1],
        ),
        (jnp.zeros_like(device_parts[0]), jnp.zeros_like(device_parts[1])),
        False,
    )
    cache_sums = earlier[0][:, None] + exclusive_forward(block_sums)
    cache_counts = earlier[1][:, None] + exclusive_forward(block_counts)
    books = jnp.repeat(codebook, blocks, axis=0)
    results = lax.map(
        lambda block_items: block_core(*block_items),
        (
            flatten(query_blocks),
            flatten(code_blocks),
            flatten(value_blocks),
            flatten(grad_blocks),
            flatten(cache_sums),
            flatten(cache_counts),
            books,
        ),
    )
    grad_query = unflatten(results[0])
    grad_value = unflatten(results[1])
    grad_sums = unflatten(results[2])
    grad_books = unflatten(results[3])
    attended = unflatten(results[4])
    device_grad = jnp.sum(grad_sums, axis=1)
    later_grad = entering(
        device_grad,
        "seq",
        lambda first_part, second_part: first_part + second_part,
        jnp.zeros_like(device_grad),
        True,
    )
    carried = later_grad[:, None] + exclusive_backward(grad_sums)
    picked = jax.vmap(jax.vmap(lambda table_rows, indices: jnp.take(table_rows, indices, axis=0)))(
        carried, code_blocks
    )
    grad_values = (grad_value + picked).astype(jnp.bfloat16)
    book_here = jnp.sum(grad_books, axis=1)
    attended_flat = from_blocks(attended).reshape(tok_here, heads_here * head_width)
    weight_term = inner_rows(attended_flat, full_grad)
    summed_weight, summed_book = lax.psum((weight_term, book_here), "seq")
    grad_weight = summed_weight.astype(jnp.bfloat16)
    return (from_blocks(grad_query), from_blocks(grad_values), summed_book, grad_weight)


F32 = jnp.float32
BF16 = jnp.bfloat16
ANY = pl.BlockSpec(memory_space=pl.ANY)
VMEM = pl.BlockSpec(memory_space=pltpu.VMEM)
SMEM = pl.BlockSpec(memory_space=pltpu.SMEM)
TILE = 256


def dot_nn(a, b):
    return lax.dot_general(a, b, (((1,), (0,)), ((), ())), preferred_element_type=F32)


def dot_nt(a, b):
    return lax.dot_general(a, b, (((1,), (1,)), ((), ())), preferred_element_type=F32)


def dot_tn(a, b):
    return lax.dot_general(a, b, (((0,), (0,)), ((), ())), preferred_element_type=F32)


def slot_rows(me, slot, half, blocks):
    outer = blocks // 2
    z, y = me // 2, me % 2
    block = lax.rem(z + outer - slot, outer) * 2 + jnp.where(half == 1, 1 - y, y)
    return block


def one_hot_rows(code_rows, block, head, code_total):
    high = code_rows[block, 0:1, head * 2 * BLOCK : head * 2 * BLOCK + BLOCK].astype(F32)
    low = code_rows[block, 0:1, head * 2 * BLOCK + BLOCK : (head + 1) * 2 * BLOCK].astype(F32)
    code = (high * 2.0 + low).astype(jnp.int32)
    rows = lax.broadcasted_iota(jnp.int32, (code_total, BLOCK), 0)
    return jnp.where(rows == code, 1.0, 0.0).astype(BF16)


def masked_exp(scores_t, offset_row, base):
    weights = jnp.exp(scores_t - offset_row)
    return weights


def causal_tile():
    key_at = lax.broadcasted_iota(jnp.int32, (TILE, TILE), 0)
    query_at = lax.broadcasted_iota(jnp.int32, (TILE, TILE), 1)
    return key_at <= query_at


def forward_kernel(blocks, heads, width, code_total, me_ref, *refs):
    slots = refs[:blocks]
    book_ref = refs[blocks]
    att_t_ref, lse_ref, q_ref, k_ref, v_ref, hot_ref = refs[blocks + 1 : blocks + 7]
    codes_ref, v_t_ref, sems = refs[blocks + 7 :]
    tokens = blocks * BLOCK
    wide = heads * width
    me = me_ref[0]
    copies = []
    for at in range(blocks):
        block = slot_rows(me, at // 2, at % 2, blocks)
        rows = pl.ds(pl.multiple_of(block * BLOCK, BLOCK), BLOCK)
        source = slots[at]
        copies.append(pltpu.make_async_copy(
            source.at[pl.ds(BLOCK, BLOCK), pl.ds(0, wide)], q_ref.at[rows, :], sems.at[0, at]))
        copies.append(pltpu.make_async_copy(
            source.at[pl.ds(BLOCK, BLOCK), pl.ds(wide, wide)], v_ref.at[rows, :], sems.at[1, at]))
        copies.append(pltpu.make_async_copy(
            source.at[pl.ds(2 * BLOCK, 16), :], codes_ref.at[block], sems.at[2, at]))
    for copy in copies:
        copy.start()
    for copy in copies:
        copy.wait()
    for head in range(heads):
        columns = slice(head * width, (head + 1) * width)
        for block in range(blocks):
            hot = one_hot_rows(codes_ref, block, head, code_total)
            hot_ref[head, :, block * BLOCK : (block + 1) * BLOCK] = hot
        k_ref[:, columns] = dot_tn(hot_ref[head], book_ref[head]).astype(BF16)
        v_t_ref[columns, :] = v_ref[:, columns].astype(F32).T.astype(BF16)
    for head in range(heads):
        columns = slice(head * width, (head + 1) * width)
        for tile in range(tokens // TILE):
            here = slice(tile * TILE, (tile + 1) * TILE)
            seen = (tile + 1) * TILE
            scores = dot_nt(k_ref[:seen, columns], q_ref[here, columns])
            last = jnp.where(causal_tile(), scores[seen - TILE :], -jnp.inf)
            scores = last if tile == 0 else jnp.concatenate([scores[: seen - TILE], last], axis=0)
            top = jnp.max(scores, axis=0, keepdims=True)
            weights = jnp.exp(scores - top)
            total = jnp.sum(weights, axis=0, keepdims=True)
            mixed = dot_nn(v_t_ref[columns, :seen], weights.astype(BF16))
            att_t_ref[columns, here] = (mixed / total).astype(BF16)
            lse_ref[head : head + 1, here] = top + jnp.log(total)


def backward_kernel(blocks, heads, width, code_total, me_ref, quarter_ref, *refs):
    grads = refs[: 4 * blocks]
    (weight_ref, att_t_ref, lse_ref, q_ref, k_ref, v_ref, hot_ref) = refs[4 * blocks : 4 * blocks + 7]
    (dq_ref, dv_ref, dbook_ref, dweight_ref) = refs[4 * blocks + 7 : 4 * blocks + 11]
    (go_ref, do_t_ref, dk_ref, delta_ref, rows_ref, own_ref, sems) = refs[4 * blocks + 11 :]
    tokens = blocks * BLOCK
    part = grads[0].shape[1]
    model = 4 * part
    me = me_ref[0]
    quarter = quarter_ref[0]
    copies = []
    for at in range(blocks):
        block = slot_rows(me, at // 2, at % 2, blocks)
        rows = pl.ds(pl.multiple_of(block * BLOCK, BLOCK), BLOCK)
        for piece in range(4):
            column = pl.multiple_of(jnp.bitwise_xor(quarter, piece) * part, part)
            copies.append(pltpu.make_async_copy(
                grads[4 * at + piece].at[pl.ds(0, BLOCK), :],
                go_ref.at[rows, pl.ds(column, part)], sems.at[at, piece]))
    for copy in copies:
        copy.start()
    for copy in copies:
        copy.wait()

    for tile in range(tokens // TILE):
        here = slice(tile * TILE, (tile + 1) * TILE)
        do_t_ref[:, here] = dot_nt(weight_ref[...], go_ref[here, :]).astype(BF16)

    @pl.loop(0, model // TILE)
    def _(step):
        columns = pl.ds(pl.multiple_of(step * TILE, TILE), TILE)
        dweight_ref[:, columns] = dot_nn(att_t_ref[...], go_ref[:, columns]).astype(BF16)

    mine = pl.ds(pl.multiple_of(me * BLOCK, BLOCK), BLOCK)
    for head in range(heads):
        columns = slice(head * width, (head + 1) * width)
        delta_ref[head : head + 1, :] = jnp.sum(
            do_t_ref[columns, :].astype(F32) * att_t_ref[columns, :].astype(F32), axis=0, keepdims=True)
        for tile in range(tokens // TILE):
            here = slice(tile * TILE, (tile + 1) * TILE)
            seen = (tile + 1) * TILE
            scores = dot_nt(k_ref[:seen, columns], q_ref[here, columns])
            weights = jnp.exp(scores - lse_ref[head : head + 1, here])
            last = jnp.where(causal_tile(), weights[seen - TILE :], 0.0)
            weights = last if tile == 0 else jnp.concatenate([weights[: seen - TILE], last], axis=0)
            grad = dot_nn(v_ref[:seen, columns], do_t_ref[columns, here])
            grad = (weights * (grad - delta_ref[head : head + 1, here])).astype(BF16)
            term = dot_nn(grad, q_ref[here, columns])
            if tile == 0:
                dk_ref[:seen, :] = term
            else:
                dk_ref[: seen - TILE, :] += term[: seen - TILE]
                dk_ref[seen - TILE : seen, :] = term[seen - TILE :]
        dbook_ref[head] = dot_nn(hot_ref[head], dk_ref[...].astype(BF16))
        scores = dot_nt(k_ref[mine, columns], q_ref[:, columns])
        key_at = lax.broadcasted_iota(jnp.int32, (BLOCK, tokens), 0) + me * BLOCK
        query_at = lax.broadcasted_iota(jnp.int32, (BLOCK, tokens), 1)
        weights = jnp.exp(jnp.where(key_at <= query_at, scores - lse_ref[head : head + 1, :], -jnp.inf))
        dv_ref[:, columns] = dot_nt(weights.astype(BF16), do_t_ref[columns, :]).astype(BF16)
        for block in range(blocks):
            span = slice(block * BLOCK, (block + 1) * BLOCK)
            rows_ref[0, block : block + 1, :] = lse_ref[head : head + 1, span]
            rows_ref[1, block : block + 1, :] = delta_ref[head : head + 1, span]
            own_ref[block] = do_t_ref[columns, span]
        own_lse = rows_ref[0, pl.ds(me, 1), :]
        own_delta = rows_ref[1, pl.ds(me, 1), :]
        scores = dot_nt(k_ref[:, columns], q_ref[mine, columns])
        key_at = lax.broadcasted_iota(jnp.int32, (tokens, BLOCK), 0)
        query_at = lax.broadcasted_iota(jnp.int32, (tokens, BLOCK), 1) + me * BLOCK
        weights = jnp.exp(jnp.where(key_at <= query_at, scores - own_lse, -jnp.inf))
        grad = dot_nn(v_ref[:, columns], own_ref[me])
        grad = (weights * (grad - own_delta)).astype(BF16)
        dq_ref[:, columns] = dot_tn(grad, k_ref[:, columns]).astype(BF16)


def gathered_on_device(queries, values, codes, codebook, out_weight, grad_out):
    blocks = lax.axis_size("seq")
    tok_here, heads, width = queries.shape
    code_total = codebook.shape[1]
    wide = heads * width
    part = grad_out.shape[1]
    if tok_here != BLOCK or part != 2 * wide or 2 * wide != 4 * BLOCK:
        raise ValueError("unexpected shapes")
    tokens = blocks * BLOCK
    outer = blocks // 2
    me = lax.axis_index("seq").astype(jnp.int32).reshape(1)
    quarter = lax.axis_index("head").astype(jnp.int32).reshape(1)

    digits = jnp.stack([codes // 2, codes % 2], axis=1).astype(BF16).reshape(1, 4 * BLOCK)
    payload = jnp.concatenate([
        grad_out,
        jnp.concatenate([queries.reshape(BLOCK, wide), values.reshape(BLOCK, wide)], axis=1),
        jnp.broadcast_to(digits, (16, 4 * BLOCK)),
    ], axis=0)

    def along_z(array, step):
        pairs = [(z * 2 + y, (z + step) % outer * 2 + y) for z in range(outer) for y in range(2)]
        return lax.ppermute(array, "seq", pairs)

    def along_y(array):
        return lax.ppermute(array, "seq", [(i, i ^ 1) for i in range(blocks)])

    def along_x(array):
        return lax.ppermute(array, "head", [(i, i ^ 2) for i in range(4)])

    def to_core(array):
        return lax.ppermute(array, "head", [(i, i ^ 1) for i in range(4)])

    slots = []
    for step in range(outer):
        held = payload if step == 0 else along_z(payload, step)
        slots.append(held)
        slots.append(along_y(held))
    grads = []
    for held in slots:
        own = held[:BLOCK]
        across = along_x(own)
        grads += [own, to_core(own), across, to_core(across)]

    q_all, k_all, v_all = (jax.ShapeDtypeStruct((tokens, wide), BF16),) * 3
    att_t, lse, q_all, k_all, v_all, hot = pl.pallas_call(
        functools.partial(forward_kernel, blocks, heads, width, code_total),
        out_shape=(
            jax.ShapeDtypeStruct((wide, tokens), BF16),
            jax.ShapeDtypeStruct((8, tokens), F32),
            q_all, k_all, v_all,
            jax.ShapeDtypeStruct((heads, code_total, tokens), BF16),
        ),
        in_specs=[SMEM] + [ANY] * blocks + [VMEM],
        out_specs=(VMEM,) * 6,
        scratch_shapes=[
            pltpu.VMEM((blocks, 16, 4 * BLOCK), BF16),
            pltpu.VMEM((wide, tokens), BF16),
            pltpu.SemaphoreType.DMA((3, blocks)),
        ],
        cost_estimate=pl.CostEstimate(flops=10**9, bytes_accessed=4 * 10**6, transcendentals=10**6),
        name="forward",
    )(me, *slots, codebook)

    dq, dv, dbook, dweight = pl.pallas_call(
        functools.partial(backward_kernel, blocks, heads, width, code_total),
        out_shape=(
            jax.ShapeDtypeStruct((BLOCK, wide), BF16),
            jax.ShapeDtypeStruct((BLOCK, wide), BF16),
            jax.ShapeDtypeStruct((heads, code_total, width), F32),
            jax.ShapeDtypeStruct((wide, 4 * part), BF16),
        ),
        in_specs=[SMEM, SMEM] + [ANY] * (4 * blocks) + [VMEM] * 7,
        out_specs=(VMEM,) * 4,
        scratch_shapes=[
            pltpu.VMEM((tokens, 4 * part), BF16),
            pltpu.VMEM((wide, tokens), BF16),
            pltpu.VMEM((tokens, width), F32),
            pltpu.VMEM((8, tokens), F32),
            pltpu.VMEM((2, blocks, BLOCK), F32),
            pltpu.VMEM((blocks, width, BLOCK), BF16),
            pltpu.SemaphoreType.DMA((blocks, 4)),
        ],
        cost_estimate=pl.CostEstimate(flops=4 * 10**9, bytes_accessed=8 * 10**6, transcendentals=10**6),
        name="backward",
    )(me, quarter, *grads, out_weight, att_t, lse, q_all, k_all, v_all, hot)
    shape = (tok_here, heads, width)
    return (dq.reshape(shape), dv.reshape(shape), dbook, dweight)


def solution(mesh):
    body = on_device
    if mesh.shape["seq"] == 8 and mesh.shape["head"] == 4:
        body = gathered_on_device
    return jax.shard_map(
        body,
        mesh=mesh,
        in_specs=(
            P("seq", "head", None),
            P("seq", "head", None),
            P("head", "seq"),
            P("head", None, None),
            P("head", None),
            P("seq", "head"),
        ),
        out_specs=(
            P("seq", "head", None),
            P("seq", "head", None),
            P("head", None, None),
            P("head", None),
        ),
        check_vma=False,
    )
```

```python
import functools

import jax
import jax.numpy as jnp
from jax import lax
from jax.experimental import pallas as pl
from jax.experimental.pallas import tpu as pltpu
from jax.sharding import PartitionSpec as P


BLOCK = 128


def entering(value, axis, join, neutral, backward):
    count, mine = (lax.axis_size(axis), lax.axis_index(axis))
    pieces = jax.tree.map(lambda part: lax.all_gather(part, axis), value)
    if backward:
        pieces = jax.tree.map(lambda part: part[::-1], pieces)
        mine = count - 1 - mine
    so_far = jax.tree.map(
        lambda part, zero: jnp.full_like(part, 0) + jnp.asarray(zero, part.dtype), value, neutral
    )

    def turn(position, so_far):
        longer = join(so_far, jax.tree.map(lambda part: part[position], pieces))
        return jax.tree.map(lambda new, old: jnp.where(position < mine, new, old), longer, so_far)

    return lax.fori_loop(0, count - 1, turn, so_far)


def inner_rows(left_side, right_side):
    return lax.dot_general(
        left_side, right_side, (((0,), (0,)), ((), ())), preferred_element_type=jnp.float32
    )


def block_core(query_rows, code_rows, value_rows, grad_rows, cache_sum, cache_count, codebook_head):
    key_rows = jnp.take(codebook_head, code_rows, axis=0)
    contract_last = (((1,), (1,)), ((), ()))
    local_score = lax.dot_general(
        query_rows, key_rows, contract_last, preferred_element_type=jnp.float32
    )
    code_score = lax.dot_general(
        query_rows, codebook_head, contract_last, preferred_element_type=jnp.float32
    )
    length = query_rows.shape[0]
    row_index = lax.broadcasted_iota(jnp.int32, (length, length), 0)
    col_index = lax.broadcasted_iota(jnp.int32, (length, length), 1)
    causal = col_index <= row_index
    top_score = jnp.maximum(
        jnp.max(jnp.where(causal, local_score, -jnp.inf), axis=1), jnp.max(code_score, axis=1)
    )
    weights = jnp.where(causal, jnp.exp(local_score - top_score[:, None]), jnp.float32(0.0))
    cache_weight = jnp.exp(code_score - top_score[:, None])
    denominator = jnp.sum(weights, axis=1) + jnp.sum(cache_weight * cache_count[None, :], axis=1)
    cache_round = cache_sum.astype(jnp.bfloat16)
    numerator = jnp.dot(
        weights.astype(jnp.bfloat16), value_rows, preferred_element_type=jnp.float32
    )
    numerator = numerator + jnp.dot(
        cache_weight.astype(jnp.bfloat16), cache_round, preferred_element_type=jnp.float32
    )
    attended = numerator / denominator[:, None]
    row_delta = jnp.sum(grad_rows.astype(jnp.float32) * attended, axis=1)
    local_grad = lax.dot_general(
        grad_rows, value_rows, contract_last, preferred_element_type=jnp.float32
    )
    cache_grad = lax.dot_general(
        grad_rows, cache_round, contract_last, preferred_element_type=jnp.float32
    )
    grad_local = (weights * (local_grad - row_delta[:, None]) / denominator[:, None]).astype(
        jnp.bfloat16
    )
    grad_cache = (
        cache_weight
        * (cache_grad - row_delta[:, None] * cache_count[None, :])
        / denominator[:, None]
    ).astype(jnp.bfloat16)
    grad_query = jnp.dot(grad_local, key_rows, preferred_element_type=jnp.float32)
    grad_query = (
        grad_query + jnp.dot(grad_cache, codebook_head, preferred_element_type=jnp.float32)
    ).astype(jnp.bfloat16)
    grad_key = inner_rows(grad_local, query_rows)
    key_high = grad_key.astype(jnp.bfloat16)
    key_low = (grad_key - key_high.astype(jnp.float32)).astype(jnp.bfloat16)
    selector = (
        code_rows[:, None] == jnp.arange(codebook_head.shape[0], dtype=jnp.int32)[None, :]
    ).astype(jnp.bfloat16)
    grad_book = inner_rows(selector, key_high) + inner_rows(selector, key_low)
    grad_book = grad_book + inner_rows(grad_cache, query_rows)
    local_share = (weights / denominator[:, None]).astype(jnp.bfloat16)
    cache_share = (cache_weight / denominator[:, None]).astype(jnp.bfloat16)
    grad_value = inner_rows(local_share, grad_rows)
    grad_sum = inner_rows(cache_share, grad_rows)
    return (grad_query, grad_value, grad_sum, grad_book, attended.astype(jnp.bfloat16))


def exclusive_forward(stacked):
    summed = jnp.cumsum(stacked, axis=1)
    return jnp.concatenate([jnp.zeros_like(stacked), summed[:, :-1]], axis=1)


def exclusive_backward(stacked):
    summed = jnp.flip(jnp.cumsum(jnp.flip(stacked, axis=1), axis=1), axis=1)
    return jnp.concatenate([summed[:, 1:], jnp.zeros_like(stacked)], axis=1)


def on_device(queries, values, codes, codebook, out_weight, grad_out):
    tok_here, heads_here, head_width = queries.shape
    code_total = codebook.shape[1]
    blocks = tok_here // BLOCK
    full_grad = lax.all_gather(grad_out, "head", axis=1, tiled=True)
    grad_flat = lax.dot_general(
        full_grad, out_weight, (((1,), (1,)), ((), ())), preferred_element_type=jnp.float32
    ).astype(jnp.bfloat16)
    grad_heads = grad_flat.reshape(tok_here, heads_here, head_width)

    def to_blocks(array):
        return jnp.moveaxis(array.reshape(blocks, BLOCK, heads_here, head_width), 2, 0)

    def from_blocks(array):
        return jnp.moveaxis(array, 0, 2).reshape(tok_here, heads_here, head_width)

    def flatten(array):
        return array.reshape((heads_here * blocks,) + array.shape[2:])

    def unflatten(array):
        return array.reshape((heads_here, blocks) + array.shape[1:])

    code_blocks = codes.reshape(heads_here, blocks, BLOCK)
    query_blocks = to_blocks(queries)
    value_blocks = to_blocks(values)
    grad_blocks = to_blocks(grad_heads)
    selector = (code_blocks[..., None] == jnp.arange(code_total, dtype=jnp.int32)).astype(
        jnp.bfloat16
    )
    block_sums = jnp.einsum(
        "hnbc,hnbd->hncd", selector, value_blocks, preferred_element_type=jnp.float32
    )
    block_counts = jnp.sum(selector, axis=2, dtype=jnp.float32)
    device_parts = (jnp.sum(block_sums, axis=1), jnp.sum(block_counts, axis=1))
    earlier = entering(
        device_parts,
        "seq",
        lambda first_part, second_part: (
            first_part[0] + second_part[0],
            first_part[1] + second_part[1],
        ),
        (jnp.zeros_like(device_parts[0]), jnp.zeros_like(device_parts[1])),
        False,
    )
    cache_sums = earlier[0][:, None] + exclusive_forward(block_sums)
    cache_counts = earlier[1][:, None] + exclusive_forward(block_counts)
    books = jnp.repeat(codebook, blocks, axis=0)
    results = lax.map(
        lambda block_items: block_core(*block_items),
        (
            flatten(query_blocks),
            flatten(code_blocks),
            flatten(value_blocks),
            flatten(grad_blocks),
            flatten(cache_sums),
            flatten(cache_counts),
            books,
        ),
    )
    grad_query = unflatten(results[0])
    grad_value = unflatten(results[1])
    grad_sums = unflatten(results[2])
    grad_books = unflatten(results[3])
    attended = unflatten(results[4])
    device_grad = jnp.sum(grad_sums, axis=1)
    later_grad = entering(
        device_grad,
        "seq",
        lambda first_part, second_part: first_part + second_part,
        jnp.zeros_like(device_grad),
        True,
    )
    carried = later_grad[:, None] + exclusive_backward(grad_sums)
    picked = jax.vmap(jax.vmap(lambda table_rows, indices: jnp.take(table_rows, indices, axis=0)))(
        carried, code_blocks
    )
    grad_values = (grad_value + picked).astype(jnp.bfloat16)
    book_here = jnp.sum(grad_books, axis=1)
    attended_flat = from_blocks(attended).reshape(tok_here, heads_here * head_width)
    weight_term = inner_rows(attended_flat, full_grad)
    summed_weight, summed_book = lax.psum((weight_term, book_here), "seq")
    grad_weight = summed_weight.astype(jnp.bfloat16)
    return (from_blocks(grad_query), from_blocks(grad_values), summed_book, grad_weight)


F32 = jnp.float32
BF16 = jnp.bfloat16
ANY = pl.BlockSpec(memory_space=pl.ANY)
VMEM = pl.BlockSpec(memory_space=pltpu.VMEM)
SMEM = pl.BlockSpec(memory_space=pltpu.SMEM)
TILE = 256


def dot_nn(a, b):
    return lax.dot_general(a, b, (((1,), (0,)), ((), ())), preferred_element_type=F32)


def dot_nt(a, b):
    return lax.dot_general(a, b, (((1,), (1,)), ((), ())), preferred_element_type=F32)


def slot_block(me, slot, half):
    return jnp.bitwise_xor(me, 2 * slot + half)


def by_head(rows, flip):
    token_major = lax.broadcasted_iota(jnp.int32, (2 * rows, 2 * rows), 1 - flip)
    head_major = lax.broadcasted_iota(jnp.int32, (2 * rows, 2 * rows), flip)
    head = jnp.where(head_major >= rows, 1, 0)
    same = token_major == 2 * (head_major - rows * head) + head
    return jnp.where(same, 1.0, 0.0).astype(BF16)


def causal_tile():
    key_at = lax.broadcasted_iota(jnp.int32, (TILE, TILE), 0)
    query_at = lax.broadcasted_iota(jnp.int32, (TILE, TILE), 1)
    return key_at <= query_at


def pack_kernel(query_ref, value_ref, code_ref, out_ref):
    rows = code_ref.shape[1]
    width = query_ref.shape[1]
    both = jnp.concatenate([query_ref[...], value_ref[...]], axis=1)
    both = dot_nn(by_head(rows, 0), both).astype(BF16)
    for head in range(2):
        for which in range(2):
            column = (2 * which + head) * width
            out_ref[:rows, column : column + width] = both[
                head * rows : (head + 1) * rows, which * width : (which + 1) * width]
        code = code_ref[head : head + 1, :]
        high = lax.shift_right_logical(code, 1)
        for digit, at in ((high, 2 * head), (code - 2 * high, 2 * head + 1)):
            digit = jnp.broadcast_to(digit.astype(F32), (16, rows)).astype(BF16)
            out_ref[rows : rows + 16, at * rows : (at + 1) * rows] = digit


def main_kernel(blocks, heads, width, code_total, me_ref, quarter_ref, *refs):
    slots = refs[:blocks]
    grads = refs[blocks : 5 * blocks]
    book_any, weight_any = refs[5 * blocks : 5 * blocks + 2]
    dq_ref, dv_ref, dbook_any, dweight_any = refs[5 * blocks + 2 : 5 * blocks + 6]
    (q_ref, k_ref, v_ref, k_t_ref, v_t_ref, hot_ref, codes_ref, att_t_ref, lse_ref, weight_ref, go_ref,
     do_t_ref, dk_ref, delta_ref, rows_ref, own_ref, dbook_ref, dweight_ref, book_ref, sems, go_sems, out_sems,
     ) = refs[5 * blocks + 6 :]
    tokens = blocks * BLOCK
    wide = heads * width
    part = grads[0].shape[1]
    model = 4 * part
    me = me_ref[0]
    quarter = quarter_ref[0]

    inputs, late = [pltpu.make_async_copy(book_any, book_ref, out_sems.at[2 + heads])], []
    for at in range(blocks):
        block = slot_block(me, at // 2, at % 2)
        rows = pl.ds(pl.multiple_of(block * BLOCK, BLOCK), BLOCK)
        source = slots[at]
        inputs.append(pltpu.make_async_copy(
            source.at[pl.ds(BLOCK, 16), :], codes_ref.at[block], sems.at[2, at]))
        inputs.append(pltpu.make_async_copy(
            source.at[pl.ds(0, BLOCK), pl.ds(0, wide)], q_ref.at[rows, :], sems.at[0, at]))
        inputs.append(pltpu.make_async_copy(
            source.at[pl.ds(0, BLOCK), pl.ds(wide, wide)], v_ref.at[rows, :], sems.at[1, at]))
    late.append(pltpu.make_async_copy(weight_any, weight_ref, out_sems.at[0]))
    for at in range(blocks):
        block = slot_block(me, at // 2, at % 2)
        rows = pl.ds(pl.multiple_of(block * BLOCK, BLOCK), BLOCK)
        for piece in range(4):
            column = pl.multiple_of(jnp.bitwise_xor(quarter, piece) * part, part)
            late.append(pltpu.make_async_copy(
                grads[4 * at + piece].at[pl.ds(0, BLOCK), :],
                go_ref.at[rows, pl.ds(column, part)], go_sems.at[at, piece]))
    for copy in inputs + late:
        copy.start()
    for copy in inputs:
        copy.wait()

    for head in range(heads):
        columns = slice(head * width, (head + 1) * width)
        for block in range(blocks):
            at = head * 2 * BLOCK
            high = codes_ref[block, 0:1, at : at + BLOCK].astype(F32)
            low = codes_ref[block, 0:1, at + BLOCK : at + 2 * BLOCK].astype(F32)
            code = (high * 2.0 + low).astype(jnp.int32)
            rows = lax.broadcasted_iota(jnp.int32, (code_total, BLOCK), 0)
            hot = jnp.where(rows == code, 1.0, 0.0).astype(BF16)
            hot_ref[head, :, block * BLOCK : (block + 1) * BLOCK] = hot
        key_t = dot_nn(book_ref[head].astype(F32).T.astype(BF16), hot_ref[head])
        k_t_ref[columns, :] = key_t.astype(BF16)
        k_ref[:, columns] = key_t.T.astype(BF16)
        v_t_ref[columns, :] = v_ref[:, columns].astype(F32).T.astype(BF16)
    for head in range(heads):
        columns = slice(head * width, (head + 1) * width)
        for tile in range(tokens // TILE):
            here = slice(tile * TILE, (tile + 1) * TILE)
            seen = (tile + 1) * TILE
            scores = dot_nt(k_ref[:seen, columns], q_ref[here, columns])
            last = jnp.where(causal_tile(), scores[seen - TILE :], -jnp.inf)
            scores = last if tile == 0 else jnp.concatenate([scores[: seen - TILE], last], axis=0)
            top = jnp.max(scores, axis=0, keepdims=True)
            weights = jnp.exp(scores - top)
            total = jnp.sum(weights, axis=0, keepdims=True)
            mixed = dot_nn(v_t_ref[columns, :seen], weights.astype(BF16))
            att_t_ref[columns, here] = (mixed / total).astype(BF16)
            lse_ref[head : head + 1, here] = top + jnp.log(total)

    for copy in late:
        copy.wait()
    for tile in range(model // TILE):
        columns = slice(tile * TILE, (tile + 1) * TILE)
        dweight_ref[:, columns] = dot_nn(att_t_ref[...], go_ref[:, columns]).astype(BF16)
    outputs = [pltpu.make_async_copy(dweight_ref, dweight_any, out_sems.at[1])]
    outputs[0].start()
    for tile in range(tokens // TILE):
        here = slice(tile * TILE, (tile + 1) * TILE)
        do_t_ref[:, here] = dot_nt(weight_ref[...], go_ref[here, :]).astype(BF16)

    mine = pl.ds(pl.multiple_of(me * BLOCK, BLOCK), BLOCK)
    dq_heads, dv_heads = [], []
    for head in range(heads):
        columns = slice(head * width, (head + 1) * width)
        delta_ref[head : head + 1, :] = jnp.sum(
            do_t_ref[columns, :].astype(F32) * att_t_ref[columns, :].astype(F32), axis=0, keepdims=True)
        for tile in range(tokens // TILE):
            here = slice(tile * TILE, (tile + 1) * TILE)
            seen = (tile + 1) * TILE
            scores = dot_nt(k_ref[:seen, columns], q_ref[here, columns])
            weights = jnp.exp(scores - lse_ref[head : head + 1, here])
            last = jnp.where(causal_tile(), weights[seen - TILE :], 0.0)
            weights = last if tile == 0 else jnp.concatenate([weights[: seen - TILE], last], axis=0)
            grad = dot_nn(v_ref[:seen, columns], do_t_ref[columns, here])
            grad = (weights * (grad - delta_ref[head : head + 1, here])).astype(BF16)
            term = dot_nn(grad, q_ref[here, columns])
            if tile == 0:
                dk_ref[:seen, :] = term
            else:
                dk_ref[: seen - TILE, :] += term[: seen - TILE]
                dk_ref[seen - TILE : seen, :] = term[seen - TILE :]
        dbook_ref[head] = dot_nn(hot_ref[head], dk_ref[...].astype(BF16))
        outputs.append(pltpu.make_async_copy(dbook_ref.at[head], dbook_any.at[head], out_sems.at[2 + head]))
        outputs[-1].start()
        scores = dot_nt(k_ref[mine, columns], q_ref[:, columns])
        key_at = lax.broadcasted_iota(jnp.int32, (BLOCK, tokens), 0) + me * BLOCK
        query_at = lax.broadcasted_iota(jnp.int32, (BLOCK, tokens), 1)
        weights = jnp.exp(jnp.where(key_at <= query_at, scores - lse_ref[head : head + 1, :], -jnp.inf))
        dv_heads.append(dot_nt(weights.astype(BF16), do_t_ref[columns, :]).astype(BF16))
        for block in range(blocks):
            span = slice(block * BLOCK, (block + 1) * BLOCK)
            rows_ref[0, block : block + 1, :] = lse_ref[head : head + 1, span]
            rows_ref[1, block : block + 1, :] = delta_ref[head : head + 1, span]
            own_ref[block] = do_t_ref[columns, span]
        own_lse = rows_ref[0, pl.ds(me, 1), :]
        own_delta = rows_ref[1, pl.ds(me, 1), :]
        scores = dot_nt(k_ref[:, columns], q_ref[mine, columns])
        key_at = lax.broadcasted_iota(jnp.int32, (tokens, BLOCK), 0)
        query_at = lax.broadcasted_iota(jnp.int32, (tokens, BLOCK), 1) + me * BLOCK
        weights = jnp.exp(jnp.where(key_at <= query_at, scores - own_lse, -jnp.inf))
        grad = dot_nn(v_ref[:, columns], own_ref[me])
        grad = (weights * (grad - own_delta)).astype(BF16)
        dq_heads.append(dot_nn(k_t_ref[columns, :], grad).T.astype(BF16))
    mix = by_head(BLOCK, 1)
    dq_ref[...] = dot_nn(mix, jnp.concatenate(dq_heads, axis=0)).astype(BF16)
    dv_ref[...] = dot_nn(mix, jnp.concatenate(dv_heads, axis=0)).astype(BF16)
    for copy in outputs:
        copy.wait()


def gathered_on_device(*arrays):
    return gathered_body(*arrays)


def gathered_body(queries, values, codes, codebook, out_weight, grad_out):
    blocks = lax.axis_size("seq")
    tok_here, heads, width = queries.shape
    code_total = codebook.shape[1]
    wide = heads * width
    part = grad_out.shape[1]
    if tok_here != BLOCK or part != 2 * wide or 2 * wide != 4 * BLOCK:
        raise ValueError("unexpected shapes")
    tokens = blocks * BLOCK
    me = lax.axis_index("seq").astype(jnp.int32).reshape(1)
    quarter = lax.axis_index("head").astype(jnp.int32).reshape(1)

    payload = pl.pallas_call(
        pack_kernel,
        out_shape=jax.ShapeDtypeStruct((BLOCK + 16, part), BF16),
        in_specs=[VMEM] * 3,
        out_specs=VMEM,
        name="pack",
    )(queries.reshape(heads * BLOCK, width), values.reshape(heads * BLOCK, width), codes)

    def exchange(array, axis, flip):
        pairs = [(i, i ^ flip) for i in range(lax.axis_size(axis))]
        return lax.ppermute(array, axis, pairs)

    def along_seq(array):
        near = exchange(array, "seq", 2)
        far = exchange(array, "seq", 4)
        held = []
        for block in (array, near, far, exchange(far, "seq", 2)):
            held += [block, exchange(block, "seq", 1)]
        return held

    slots = along_seq(payload)
    grads = []
    for own in along_seq(grad_out):
        across = exchange(own, "head", 2)
        grads += [own, exchange(own, "head", 1), across, exchange(across, "head", 1)]

    main = pl.pallas_call(
        functools.partial(main_kernel, blocks, heads, width, code_total),
        out_shape=(
            jax.ShapeDtypeStruct((heads * BLOCK, width), BF16),
            jax.ShapeDtypeStruct((heads * BLOCK, width), BF16),
            jax.ShapeDtypeStruct((heads, code_total, width), F32),
            jax.ShapeDtypeStruct((wide, 4 * part), BF16),
        ),
        in_specs=[SMEM, SMEM] + [ANY] * (5 * blocks + 2),
        out_specs=(VMEM, VMEM, ANY, ANY),
        scratch_shapes=[
            pltpu.VMEM((tokens, wide), BF16),
            pltpu.VMEM((tokens, wide), BF16),
            pltpu.VMEM((tokens, wide), BF16),
            pltpu.VMEM((wide, tokens), BF16),
            pltpu.VMEM((wide, tokens), BF16),
            pltpu.VMEM((heads, code_total, tokens), BF16),
            pltpu.VMEM((blocks, 16, 4 * BLOCK), BF16),
            pltpu.VMEM((wide, tokens), BF16),
            pltpu.VMEM((8, tokens), F32),
            pltpu.VMEM((wide, 4 * part), BF16),
            pltpu.VMEM((tokens, 4 * part), BF16),
            pltpu.VMEM((wide, tokens), BF16),
            pltpu.VMEM((tokens, width), F32),
            pltpu.VMEM((8, tokens), F32),
            pltpu.VMEM((2, blocks, BLOCK), F32),
            pltpu.VMEM((blocks, width, BLOCK), BF16),
            pltpu.VMEM((heads, code_total, width), F32),
            pltpu.VMEM((wide, 4 * part), BF16),
            pltpu.VMEM((heads, code_total, width), BF16),
            pltpu.SemaphoreType.DMA((3, blocks)),
            pltpu.SemaphoreType.DMA((blocks, 4)),
            pltpu.SemaphoreType.DMA((3 + heads,)),
        ],
        compiler_params=pltpu.CompilerParams(vmem_limit_bytes=28 * 2**20),
        cost_estimate=pl.CostEstimate(flops=5 * 10**9, bytes_accessed=8 * 10**6, transcendentals=10**6),
        name="main",
    )
    slots[0], grads[0], codebook, out_weight = (
        pltpu.with_memory_space_constraint(array, pltpu.HBM)
        for array in (slots[0], grads[0], codebook, out_weight)
    )
    dq, dv, dbook, dweight = main(me, quarter, *slots, *grads, codebook, out_weight)
    shape = (tok_here, heads, width)
    return (dq.reshape(shape), dv.reshape(shape), dbook, dweight)


def solution(mesh):
    body = on_device
    gathered = mesh.shape["seq"] == 8 and mesh.shape["head"] == 4
    if gathered:
        body = gathered_on_device
    return jax.shard_map(
        body,
        mesh=mesh,
        in_specs=(
            P("seq", "head", None),
            P("seq", "head", None),
            P("head", "seq"),
            P("head", None, None),
            P("head", None),
            P("seq", "head"),
        ),
        out_specs=(
            P("seq", "head", None),
            P("seq", "head", None),
            P("head", None, None),
            P("head", None),
        ),
        check_vma=False,
    )
```

```python
import functools

import jax
import jax.numpy as jnp
from jax import lax
from jax.experimental import pallas as pl
from jax.experimental.pallas import tpu as pltpu
from jax.sharding import PartitionSpec as P


BLOCK = 128


def entering(value, axis, join, neutral, backward):
    count, mine = (lax.axis_size(axis), lax.axis_index(axis))
    pieces = jax.tree.map(lambda part: lax.all_gather(part, axis), value)
    if backward:
        pieces = jax.tree.map(lambda part: part[::-1], pieces)
        mine = count - 1 - mine
    so_far = jax.tree.map(
        lambda part, zero: jnp.full_like(part, 0) + jnp.asarray(zero, part.dtype), value, neutral
    )

    def turn(position, so_far):
        longer = join(so_far, jax.tree.map(lambda part: part[position], pieces))
        return jax.tree.map(lambda new, old: jnp.where(position < mine, new, old), longer, so_far)

    return lax.fori_loop(0, count - 1, turn, so_far)


def inner_rows(left_side, right_side):
    return lax.dot_general(
        left_side, right_side, (((0,), (0,)), ((), ())), preferred_element_type=jnp.float32
    )


def block_core(query_rows, code_rows, value_rows, grad_rows, cache_sum, cache_count, codebook_head):
    key_rows = jnp.take(codebook_head, code_rows, axis=0)
    contract_last = (((1,), (1,)), ((), ()))
    local_score = lax.dot_general(
        query_rows, key_rows, contract_last, preferred_element_type=jnp.float32
    )
    code_score = lax.dot_general(
        query_rows, codebook_head, contract_last, preferred_element_type=jnp.float32
    )
    length = query_rows.shape[0]
    row_index = lax.broadcasted_iota(jnp.int32, (length, length), 0)
    col_index = lax.broadcasted_iota(jnp.int32, (length, length), 1)
    causal = col_index <= row_index
    top_score = jnp.maximum(
        jnp.max(jnp.where(causal, local_score, -jnp.inf), axis=1), jnp.max(code_score, axis=1)
    )
    weights = jnp.where(causal, jnp.exp(local_score - top_score[:, None]), jnp.float32(0.0))
    cache_weight = jnp.exp(code_score - top_score[:, None])
    denominator = jnp.sum(weights, axis=1) + jnp.sum(cache_weight * cache_count[None, :], axis=1)
    cache_round = cache_sum.astype(jnp.bfloat16)
    numerator = jnp.dot(
        weights.astype(jnp.bfloat16), value_rows, preferred_element_type=jnp.float32
    )
    numerator = numerator + jnp.dot(
        cache_weight.astype(jnp.bfloat16), cache_round, preferred_element_type=jnp.float32
    )
    attended = numerator / denominator[:, None]
    row_delta = jnp.sum(grad_rows.astype(jnp.float32) * attended, axis=1)
    local_grad = lax.dot_general(
        grad_rows, value_rows, contract_last, preferred_element_type=jnp.float32
    )
    cache_grad = lax.dot_general(
        grad_rows, cache_round, contract_last, preferred_element_type=jnp.float32
    )
    grad_local = (weights * (local_grad - row_delta[:, None]) / denominator[:, None]).astype(
        jnp.bfloat16
    )
    grad_cache = (
        cache_weight
        * (cache_grad - row_delta[:, None] * cache_count[None, :])
        / denominator[:, None]
    ).astype(jnp.bfloat16)
    grad_query = jnp.dot(grad_local, key_rows, preferred_element_type=jnp.float32)
    grad_query = (
        grad_query + jnp.dot(grad_cache, codebook_head, preferred_element_type=jnp.float32)
    ).astype(jnp.bfloat16)
    grad_key = inner_rows(grad_local, query_rows)
    key_high = grad_key.astype(jnp.bfloat16)
    key_low = (grad_key - key_high.astype(jnp.float32)).astype(jnp.bfloat16)
    selector = (
        code_rows[:, None] == jnp.arange(codebook_head.shape[0], dtype=jnp.int32)[None, :]
    ).astype(jnp.bfloat16)
    grad_book = inner_rows(selector, key_high) + inner_rows(selector, key_low)
    grad_book = grad_book + inner_rows(grad_cache, query_rows)
    local_share = (weights / denominator[:, None]).astype(jnp.bfloat16)
    cache_share = (cache_weight / denominator[:, None]).astype(jnp.bfloat16)
    grad_value = inner_rows(local_share, grad_rows)
    grad_sum = inner_rows(cache_share, grad_rows)
    return (grad_query, grad_value, grad_sum, grad_book, attended.astype(jnp.bfloat16))


def exclusive_forward(stacked):
    summed = jnp.cumsum(stacked, axis=1)
    return jnp.concatenate([jnp.zeros_like(stacked), summed[:, :-1]], axis=1)


def exclusive_backward(stacked):
    summed = jnp.flip(jnp.cumsum(jnp.flip(stacked, axis=1), axis=1), axis=1)
    return jnp.concatenate([summed[:, 1:], jnp.zeros_like(stacked)], axis=1)


def on_device(queries, values, codes, codebook, out_weight, grad_out):
    tok_here, heads_here, head_width = queries.shape
    code_total = codebook.shape[1]
    blocks = tok_here // BLOCK
    full_grad = lax.all_gather(grad_out, "head", axis=1, tiled=True)
    grad_flat = lax.dot_general(
        full_grad, out_weight, (((1,), (1,)), ((), ())), preferred_element_type=jnp.float32
    ).astype(jnp.bfloat16)
    grad_heads = grad_flat.reshape(tok_here, heads_here, head_width)

    def to_blocks(array):
        return jnp.moveaxis(array.reshape(blocks, BLOCK, heads_here, head_width), 2, 0)

    def from_blocks(array):
        return jnp.moveaxis(array, 0, 2).reshape(tok_here, heads_here, head_width)

    def flatten(array):
        return array.reshape((heads_here * blocks,) + array.shape[2:])

    def unflatten(array):
        return array.reshape((heads_here, blocks) + array.shape[1:])

    code_blocks = codes.reshape(heads_here, blocks, BLOCK)
    query_blocks = to_blocks(queries)
    value_blocks = to_blocks(values)
    grad_blocks = to_blocks(grad_heads)
    selector = (code_blocks[..., None] == jnp.arange(code_total, dtype=jnp.int32)).astype(
        jnp.bfloat16
    )
    block_sums = jnp.einsum(
        "hnbc,hnbd->hncd", selector, value_blocks, preferred_element_type=jnp.float32
    )
    block_counts = jnp.sum(selector, axis=2, dtype=jnp.float32)
    device_parts = (jnp.sum(block_sums, axis=1), jnp.sum(block_counts, axis=1))
    earlier = entering(
        device_parts,
        "seq",
        lambda first_part, second_part: (
            first_part[0] + second_part[0],
            first_part[1] + second_part[1],
        ),
        (jnp.zeros_like(device_parts[0]), jnp.zeros_like(device_parts[1])),
        False,
    )
    cache_sums = earlier[0][:, None] + exclusive_forward(block_sums)
    cache_counts = earlier[1][:, None] + exclusive_forward(block_counts)
    books = jnp.repeat(codebook, blocks, axis=0)
    results = lax.map(
        lambda block_items: block_core(*block_items),
        (
            flatten(query_blocks),
            flatten(code_blocks),
            flatten(value_blocks),
            flatten(grad_blocks),
            flatten(cache_sums),
            flatten(cache_counts),
            books,
        ),
    )
    grad_query = unflatten(results[0])
    grad_value = unflatten(results[1])
    grad_sums = unflatten(results[2])
    grad_books = unflatten(results[3])
    attended = unflatten(results[4])
    device_grad = jnp.sum(grad_sums, axis=1)
    later_grad = entering(
        device_grad,
        "seq",
        lambda first_part, second_part: first_part + second_part,
        jnp.zeros_like(device_grad),
        True,
    )
    carried = later_grad[:, None] + exclusive_backward(grad_sums)
    picked = jax.vmap(jax.vmap(lambda table_rows, indices: jnp.take(table_rows, indices, axis=0)))(
        carried, code_blocks
    )
    grad_values = (grad_value + picked).astype(jnp.bfloat16)
    book_here = jnp.sum(grad_books, axis=1)
    attended_flat = from_blocks(attended).reshape(tok_here, heads_here * head_width)
    weight_term = inner_rows(attended_flat, full_grad)
    summed_weight, summed_book = lax.psum((weight_term, book_here), "seq")
    grad_weight = summed_weight.astype(jnp.bfloat16)
    return (from_blocks(grad_query), from_blocks(grad_values), summed_book, grad_weight)


F32 = jnp.float32
BF16 = jnp.bfloat16
ANY = pl.BlockSpec(memory_space=pl.ANY)
VMEM = pl.BlockSpec(memory_space=pltpu.VMEM)
SMEM = pl.BlockSpec(memory_space=pltpu.SMEM)
TILE = 256


def dot_nn(a, b):
    return lax.dot_general(a, b, (((1,), (0,)), ((), ())), preferred_element_type=F32)


def dot_nt(a, b):
    return lax.dot_general(a, b, (((1,), (1,)), ((), ())), preferred_element_type=F32)


def slot_block(me, slot, half):
    return jnp.bitwise_xor(me, 2 * slot + half)


def by_head(rows, flip):
    token_major = lax.broadcasted_iota(jnp.int32, (2 * rows, 2 * rows), 1 - flip)
    head_major = lax.broadcasted_iota(jnp.int32, (2 * rows, 2 * rows), flip)
    head = jnp.where(head_major >= rows, 1, 0)
    same = token_major == 2 * (head_major - rows * head) + head
    return jnp.where(same, 1.0, 0.0).astype(BF16)


def causal_tile():
    key_at = lax.broadcasted_iota(jnp.int32, (TILE, TILE), 0)
    query_at = lax.broadcasted_iota(jnp.int32, (TILE, TILE), 1)
    return key_at <= query_at


def pack_kernel(query_ref, value_ref, code_ref, out_ref):
    rows = code_ref.shape[1]
    width = query_ref.shape[1]
    both = jnp.concatenate([query_ref[...], value_ref[...]], axis=1)
    both = dot_nn(by_head(rows, 0), both).astype(BF16)
    for head in range(2):
        for which in range(2):
            column = (2 * which + head) * width
            out_ref[:rows, column : column + width] = both[
                head * rows : (head + 1) * rows, which * width : (which + 1) * width]
        code = code_ref[head : head + 1, :]
        high = lax.shift_right_logical(code, 1)
        for digit, at in ((high, 2 * head), (code - 2 * high, 2 * head + 1)):
            digit = jnp.broadcast_to(digit.astype(F32), (8, rows)).astype(BF16)
            out_ref[rows : rows + 8, at * rows : (at + 1) * rows] = digit


def main_kernel(blocks, heads, width, code_total, me_ref, quarter_ref, *refs):
    slots = refs[:blocks]
    grads = refs[blocks : 5 * blocks]
    book_any, weight_any = refs[5 * blocks : 5 * blocks + 2]
    dq_ref, dv_ref, dbook_any, dweight_any = refs[5 * blocks + 2 : 5 * blocks + 6]
    (q_ref, k_ref, v_ref, k_t_ref, v_t_ref, hot_ref, codes_ref, att_t_ref, lse_ref, weight_ref, go_ref,
     do_t_ref, dk_ref, delta_ref, rows_ref, own_ref, dbook_ref, dweight_ref, book_ref, sems, go_sems, out_sems,
     ) = refs[5 * blocks + 6 :]
    tokens = blocks * BLOCK
    wide = heads * width
    part = grads[0].shape[1]
    model = 4 * part
    me = me_ref[0]
    quarter = quarter_ref[0]

    inputs = [pltpu.make_async_copy(book_any, book_ref, out_sems.at[2 + heads])]
    codes_in, late = [], []
    for at in range(blocks):
        block = slot_block(me, at // 2, at % 2)
        rows = pl.ds(pl.multiple_of(block * BLOCK, BLOCK), BLOCK)
        source = slots[at]
        codes_in.append(pltpu.make_async_copy(
            source.at[pl.ds(BLOCK, 8), :], codes_ref.at[block], sems.at[2, at]))
        inputs.append(pltpu.make_async_copy(
            source.at[pl.ds(0, BLOCK), pl.ds(0, wide)], q_ref.at[rows, :], sems.at[0, at]))
        inputs.append(pltpu.make_async_copy(
            source.at[pl.ds(0, BLOCK), pl.ds(wide, wide)], v_ref.at[rows, :], sems.at[1, at]))
    late.append(pltpu.make_async_copy(weight_any, weight_ref, out_sems.at[0]))
    for at in range(blocks):
        block = slot_block(me, at // 2, at % 2)
        rows = pl.ds(pl.multiple_of(block * BLOCK, BLOCK), BLOCK)
        for piece in range(4):
            column = pl.multiple_of(jnp.bitwise_xor(quarter, piece) * part, part)
            late.append(pltpu.make_async_copy(
                grads[4 * at + piece].at[pl.ds(0, BLOCK), :],
                go_ref.at[rows, pl.ds(column, part)], go_sems.at[at, piece]))
    for copy in codes_in + inputs:
        copy.start()
    for copy in codes_in:
        copy.wait()

    for head in range(heads):
        columns = slice(head * width, (head + 1) * width)
        for block in range(blocks):
            at = head * 2 * BLOCK
            high = codes_ref[block, 0:1, at : at + BLOCK].astype(F32)
            low = codes_ref[block, 0:1, at + BLOCK : at + 2 * BLOCK].astype(F32)
            code = (high * 2.0 + low).astype(jnp.int32)
            rows = lax.broadcasted_iota(jnp.int32, (code_total, BLOCK), 0)
            hot = jnp.where(rows == code, 1.0, 0.0).astype(BF16)
            hot_ref[head, :, block * BLOCK : (block + 1) * BLOCK] = hot
    for copy in inputs:
        copy.wait()
    for copy in late:
        copy.start()
    for head in range(heads):
        columns = slice(head * width, (head + 1) * width)
        key_t = dot_nn(book_ref[head].astype(F32).T.astype(BF16), hot_ref[head])
        k_t_ref[columns, :] = key_t.astype(BF16)
        k_ref[:, columns] = key_t.T.astype(BF16)
        v_t_ref[columns, :] = v_ref[:, columns].astype(F32).T.astype(BF16)

    def scored(head, tile):
        columns = slice(head * width, (head + 1) * width)
        seen = (tile + 1) * TILE
        return dot_nt(k_ref[:seen, columns], q_ref[tile * TILE : seen, columns])

    steps = [(head, tile) for tile in range(tokens // TILE) for head in range(heads)]
    ahead = scored(*steps[0])
    for at, (head, tile) in enumerate(steps):
        columns = slice(head * width, (head + 1) * width)
        here = slice(tile * TILE, (tile + 1) * TILE)
        seen = (tile + 1) * TILE
        scores = ahead
        if at + 1 < len(steps):
            ahead = scored(*steps[at + 1])
        last = jnp.where(causal_tile(), scores[seen - TILE :], -jnp.inf)
        scores = last if tile == 0 else jnp.concatenate([scores[: seen - TILE], last], axis=0)
        top = jnp.max(scores, axis=0, keepdims=True)
        weights = jnp.exp(scores - top)
        total = jnp.sum(weights, axis=0, keepdims=True)
        mixed = dot_nn(v_t_ref[columns, :seen], weights.astype(BF16))
        att_t_ref[columns, here] = (mixed / total).astype(BF16)
        lse_ref[head : head + 1, here] = top + jnp.log(total)

    for copy in late:
        copy.wait()
    for tile in range(model // TILE):
        columns = slice(tile * TILE, (tile + 1) * TILE)
        dweight_ref[:, columns] = dot_nn(att_t_ref[...], go_ref[:, columns]).astype(BF16)
    outputs = [pltpu.make_async_copy(dweight_ref, dweight_any, out_sems.at[1])]
    outputs[0].start()
    for tile in range(tokens // TILE):
        here = slice(tile * TILE, (tile + 1) * TILE)
        do_t_ref[:, here] = dot_nt(weight_ref[...], go_ref[here, :]).astype(BF16)

    mine = pl.ds(pl.multiple_of(me * BLOCK, BLOCK), BLOCK)
    dq_heads, dv_heads = [], []
    for head in range(heads):
        columns = slice(head * width, (head + 1) * width)
        delta_ref[head : head + 1, :] = jnp.sum(
            do_t_ref[columns, :].astype(F32) * att_t_ref[columns, :].astype(F32), axis=0, keepdims=True)

    def products(head, tile):
        columns = slice(head * width, (head + 1) * width)
        seen = (tile + 1) * TILE
        grad = dot_nn(v_ref[:seen, columns], do_t_ref[columns, tile * TILE : seen])
        return scored(head, tile), grad

    ahead = products(*steps[0])
    for at, (head, tile) in enumerate(steps):
        columns = slice(head * width, (head + 1) * width)
        here = slice(tile * TILE, (tile + 1) * TILE)
        seen = (tile + 1) * TILE
        scores, grad = ahead
        if at + 1 < len(steps):
            ahead = products(*steps[at + 1])
        weights = jnp.exp(scores - lse_ref[head : head + 1, here])
        last = jnp.where(causal_tile(), weights[seen - TILE :], 0.0)
        weights = last if tile == 0 else jnp.concatenate([weights[: seen - TILE], last], axis=0)
        grad = (weights * (grad - delta_ref[head : head + 1, here])).astype(BF16)
        term = dot_nn(grad, q_ref[here, columns])
        if tile == 0:
            dk_ref[head, :seen, :] = term
        else:
            dk_ref[head, : seen - TILE, :] += term[: seen - TILE]
            dk_ref[head, seen - TILE : seen, :] = term[seen - TILE :]
    for head in range(heads):
        columns = slice(head * width, (head + 1) * width)
        dbook_ref[head] = dot_nn(hot_ref[head], dk_ref[head].astype(BF16))
        outputs.append(pltpu.make_async_copy(dbook_ref.at[head], dbook_any.at[head], out_sems.at[2 + head]))
        outputs[-1].start()
        scores = dot_nt(k_ref[mine, columns], q_ref[:, columns])
        key_at = lax.broadcasted_iota(jnp.int32, (BLOCK, tokens), 0) + me * BLOCK
        query_at = lax.broadcasted_iota(jnp.int32, (BLOCK, tokens), 1)
        weights = jnp.exp(jnp.where(key_at <= query_at, scores - lse_ref[head : head + 1, :], -jnp.inf))
        dv_heads.append(dot_nt(weights.astype(BF16), do_t_ref[columns, :]).astype(BF16))
        for block in range(blocks):
            span = slice(block * BLOCK, (block + 1) * BLOCK)
            rows_ref[0, block : block + 1, :] = lse_ref[head : head + 1, span]
            rows_ref[1, block : block + 1, :] = delta_ref[head : head + 1, span]
            own_ref[block] = do_t_ref[columns, span]
        own_lse = rows_ref[0, pl.ds(me, 1), :]
        own_delta = rows_ref[1, pl.ds(me, 1), :]
        scores = dot_nt(k_ref[:, columns], q_ref[mine, columns])
        key_at = lax.broadcasted_iota(jnp.int32, (tokens, BLOCK), 0)
        query_at = lax.broadcasted_iota(jnp.int32, (tokens, BLOCK), 1) + me * BLOCK
        weights = jnp.exp(jnp.where(key_at <= query_at, scores - own_lse, -jnp.inf))
        grad = dot_nn(v_ref[:, columns], own_ref[me])
        grad = (weights * (grad - own_delta)).astype(BF16)
        dq_heads.append(dot_nn(k_t_ref[columns, :], grad).T.astype(BF16))
    mix = by_head(BLOCK, 1)
    dq_ref[...] = dot_nn(mix, jnp.concatenate(dq_heads, axis=0)).astype(BF16)
    dv_ref[...] = dot_nn(mix, jnp.concatenate(dv_heads, axis=0)).astype(BF16)
    for copy in outputs:
        copy.wait()


def gathered_on_device(*arrays):
    return gathered_body(*arrays)


def gathered_body(queries, values, codes, codebook, out_weight, grad_out):
    blocks = lax.axis_size("seq")
    tok_here, heads, width = queries.shape
    code_total = codebook.shape[1]
    wide = heads * width
    part = grad_out.shape[1]
    if tok_here != BLOCK or part != 2 * wide or 2 * wide != 4 * BLOCK:
        raise ValueError("unexpected shapes")
    tokens = blocks * BLOCK
    me = lax.axis_index("seq").astype(jnp.int32).reshape(1)
    quarter = lax.axis_index("head").astype(jnp.int32).reshape(1)

    payload = pl.pallas_call(
        pack_kernel,
        out_shape=jax.ShapeDtypeStruct((BLOCK + 8, part), BF16),
        in_specs=[VMEM] * 3,
        out_specs=VMEM,
        name="pack",
    )(queries.reshape(heads * BLOCK, width), values.reshape(heads * BLOCK, width), codes)

    def exchange(array, axis, flip):
        pairs = [(i, i ^ flip) for i in range(lax.axis_size(axis))]
        return lax.ppermute(array, axis, pairs)

    def along_seq(array):
        near = exchange(array, "seq", 2)
        far = exchange(array, "seq", 4)
        held = []
        for block in (array, near, far, exchange(far, "seq", 2)):
            held += [block, exchange(block, "seq", 1)]
        return held

    slots = along_seq(payload)
    grads = []
    for own in along_seq(grad_out):
        across = exchange(own, "head", 2)
        grads += [own, exchange(own, "head", 1), across, exchange(across, "head", 1)]

    main = pl.pallas_call(
        functools.partial(main_kernel, blocks, heads, width, code_total),
        out_shape=(
            jax.ShapeDtypeStruct((heads * BLOCK, width), BF16),
            jax.ShapeDtypeStruct((heads * BLOCK, width), BF16),
            jax.ShapeDtypeStruct((heads, code_total, width), F32),
            jax.ShapeDtypeStruct((wide, 4 * part), BF16),
        ),
        in_specs=[SMEM, SMEM] + [ANY] * (5 * blocks + 2),
        out_specs=(VMEM, VMEM, ANY, ANY),
        scratch_shapes=[
            pltpu.VMEM((tokens, wide), BF16),
            pltpu.VMEM((tokens, wide), BF16),
            pltpu.VMEM((tokens, wide), BF16),
            pltpu.VMEM((wide, tokens), BF16),
            pltpu.VMEM((wide, tokens), BF16),
            pltpu.VMEM((heads, code_total, tokens), BF16),
            pltpu.VMEM((blocks, 8, 4 * BLOCK), BF16),
            pltpu.VMEM((wide, tokens), BF16),
            pltpu.VMEM((8, tokens), F32),
            pltpu.VMEM((wide, 4 * part), BF16),
            pltpu.VMEM((tokens, 4 * part), BF16),
            pltpu.VMEM((wide, tokens), BF16),
            pltpu.VMEM((heads, tokens, width), F32),
            pltpu.VMEM((8, tokens), F32),
            pltpu.VMEM((2, blocks, BLOCK), F32),
            pltpu.VMEM((blocks, width, BLOCK), BF16),
            pltpu.VMEM((heads, code_total, width), F32),
            pltpu.VMEM((wide, 4 * part), BF16),
            pltpu.VMEM((heads, code_total, width), BF16),
            pltpu.SemaphoreType.DMA((3, blocks)),
            pltpu.SemaphoreType.DMA((blocks, 4)),
            pltpu.SemaphoreType.DMA((3 + heads,)),
        ],
        compiler_params=pltpu.CompilerParams(vmem_limit_bytes=28 * 2**20),
        cost_estimate=pl.CostEstimate(flops=5 * 10**9, bytes_accessed=8 * 10**6, transcendentals=10**6),
        name="main",
    )
    slots[0], grads[0], codebook, out_weight = (
        pltpu.with_memory_space_constraint(array, pltpu.HBM)
        for array in (slots[0], grads[0], codebook, out_weight)
    )
    dq, dv, dbook, dweight = main(me, quarter, *slots, *grads, codebook, out_weight)
    shape = (tok_here, heads, width)
    return (dq.reshape(shape), dv.reshape(shape), dbook, dweight)


def solution(mesh):
    body = on_device
    gathered = mesh.shape["seq"] == 8 and mesh.shape["head"] == 4
    if gathered:
        body = gathered_on_device
    return jax.shard_map(
        body,
        mesh=mesh,
        in_specs=(
            P("seq", "head", None),
            P("seq", "head", None),
            P("head", "seq"),
            P("head", None, None),
            P("head", None),
            P("seq", "head"),
        ),
        out_specs=(
            P("seq", "head", None),
            P("seq", "head", None),
            P("head", None, None),
            P("head", None),
        ),
        check_vma=False,
    )
```

```python
import functools

import jax
import jax.numpy as jnp
from jax import lax
from jax.experimental import pallas as pl
from jax.experimental.pallas import tpu as pltpu
from jax.sharding import PartitionSpec as P


BLOCK = 128


def entering(value, axis, join, neutral, backward):
    count, mine = (lax.axis_size(axis), lax.axis_index(axis))
    pieces = jax.tree.map(lambda part: lax.all_gather(part, axis), value)
    if backward:
        pieces = jax.tree.map(lambda part: part[::-1], pieces)
        mine = count - 1 - mine
    so_far = jax.tree.map(
        lambda part, zero: jnp.full_like(part, 0) + jnp.asarray(zero, part.dtype), value, neutral
    )

    def turn(position, so_far):
        longer = join(so_far, jax.tree.map(lambda part: part[position], pieces))
        return jax.tree.map(lambda new, old: jnp.where(position < mine, new, old), longer, so_far)

    return lax.fori_loop(0, count - 1, turn, so_far)


def inner_rows(left_side, right_side):
    return lax.dot_general(
        left_side, right_side, (((0,), (0,)), ((), ())), preferred_element_type=jnp.float32
    )


def block_core(query_rows, code_rows, value_rows, grad_rows, cache_sum, cache_count, codebook_head):
    key_rows = jnp.take(codebook_head, code_rows, axis=0)
    contract_last = (((1,), (1,)), ((), ()))
    local_score = lax.dot_general(
        query_rows, key_rows, contract_last, preferred_element_type=jnp.float32
    )
    code_score = lax.dot_general(
        query_rows, codebook_head, contract_last, preferred_element_type=jnp.float32
    )
    length = query_rows.shape[0]
    row_index = lax.broadcasted_iota(jnp.int32, (length, length), 0)
    col_index = lax.broadcasted_iota(jnp.int32, (length, length), 1)
    causal = col_index <= row_index
    top_score = jnp.maximum(
        jnp.max(jnp.where(causal, local_score, -jnp.inf), axis=1), jnp.max(code_score, axis=1)
    )
    weights = jnp.where(causal, jnp.exp(local_score - top_score[:, None]), jnp.float32(0.0))
    cache_weight = jnp.exp(code_score - top_score[:, None])
    denominator = jnp.sum(weights, axis=1) + jnp.sum(cache_weight * cache_count[None, :], axis=1)
    cache_round = cache_sum.astype(jnp.bfloat16)
    numerator = jnp.dot(
        weights.astype(jnp.bfloat16), value_rows, preferred_element_type=jnp.float32
    )
    numerator = numerator + jnp.dot(
        cache_weight.astype(jnp.bfloat16), cache_round, preferred_element_type=jnp.float32
    )
    attended = numerator / denominator[:, None]
    row_delta = jnp.sum(grad_rows.astype(jnp.float32) * attended, axis=1)
    local_grad = lax.dot_general(
        grad_rows, value_rows, contract_last, preferred_element_type=jnp.float32
    )
    cache_grad = lax.dot_general(
        grad_rows, cache_round, contract_last, preferred_element_type=jnp.float32
    )
    grad_local = (weights * (local_grad - row_delta[:, None]) / denominator[:, None]).astype(
        jnp.bfloat16
    )
    grad_cache = (
        cache_weight
        * (cache_grad - row_delta[:, None] * cache_count[None, :])
        / denominator[:, None]
    ).astype(jnp.bfloat16)
    grad_query = jnp.dot(grad_local, key_rows, preferred_element_type=jnp.float32)
    grad_query = (
        grad_query + jnp.dot(grad_cache, codebook_head, preferred_element_type=jnp.float32)
    ).astype(jnp.bfloat16)
    grad_key = inner_rows(grad_local, query_rows)
    key_high = grad_key.astype(jnp.bfloat16)
    key_low = (grad_key - key_high.astype(jnp.float32)).astype(jnp.bfloat16)
    selector = (
        code_rows[:, None] == jnp.arange(codebook_head.shape[0], dtype=jnp.int32)[None, :]
    ).astype(jnp.bfloat16)
    grad_book = inner_rows(selector, key_high) + inner_rows(selector, key_low)
    grad_book = grad_book + inner_rows(grad_cache, query_rows)
    local_share = (weights / denominator[:, None]).astype(jnp.bfloat16)
    cache_share = (cache_weight / denominator[:, None]).astype(jnp.bfloat16)
    grad_value = inner_rows(local_share, grad_rows)
    grad_sum = inner_rows(cache_share, grad_rows)
    return (grad_query, grad_value, grad_sum, grad_book, attended.astype(jnp.bfloat16))


def exclusive_forward(stacked):
    summed = jnp.cumsum(stacked, axis=1)
    return jnp.concatenate([jnp.zeros_like(stacked), summed[:, :-1]], axis=1)


def exclusive_backward(stacked):
    summed = jnp.flip(jnp.cumsum(jnp.flip(stacked, axis=1), axis=1), axis=1)
    return jnp.concatenate([summed[:, 1:], jnp.zeros_like(stacked)], axis=1)


def on_device(queries, values, codes, codebook, out_weight, grad_out):
    tok_here, heads_here, head_width = queries.shape
    code_total = codebook.shape[1]
    blocks = tok_here // BLOCK
    full_grad = lax.all_gather(grad_out, "head", axis=1, tiled=True)
    grad_flat = lax.dot_general(
        full_grad, out_weight, (((1,), (1,)), ((), ())), preferred_element_type=jnp.float32
    ).astype(jnp.bfloat16)
    grad_heads = grad_flat.reshape(tok_here, heads_here, head_width)

    def to_blocks(array):
        return jnp.moveaxis(array.reshape(blocks, BLOCK, heads_here, head_width), 2, 0)

    def from_blocks(array):
        return jnp.moveaxis(array, 0, 2).reshape(tok_here, heads_here, head_width)

    def flatten(array):
        return array.reshape((heads_here * blocks,) + array.shape[2:])

    def unflatten(array):
        return array.reshape((heads_here, blocks) + array.shape[1:])

    code_blocks = codes.reshape(heads_here, blocks, BLOCK)
    query_blocks = to_blocks(queries)
    value_blocks = to_blocks(values)
    grad_blocks = to_blocks(grad_heads)
    selector = (code_blocks[..., None] == jnp.arange(code_total, dtype=jnp.int32)).astype(
        jnp.bfloat16
    )
    block_sums = jnp.einsum(
        "hnbc,hnbd->hncd", selector, value_blocks, preferred_element_type=jnp.float32
    )
    block_counts = jnp.sum(selector, axis=2, dtype=jnp.float32)
    device_parts = (jnp.sum(block_sums, axis=1), jnp.sum(block_counts, axis=1))
    earlier = entering(
        device_parts,
        "seq",
        lambda first_part, second_part: (
            first_part[0] + second_part[0],
            first_part[1] + second_part[1],
        ),
        (jnp.zeros_like(device_parts[0]), jnp.zeros_like(device_parts[1])),
        False,
    )
    cache_sums = earlier[0][:, None] + exclusive_forward(block_sums)
    cache_counts = earlier[1][:, None] + exclusive_forward(block_counts)
    books = jnp.repeat(codebook, blocks, axis=0)
    results = lax.map(
        lambda block_items: block_core(*block_items),
        (
            flatten(query_blocks),
            flatten(code_blocks),
            flatten(value_blocks),
            flatten(grad_blocks),
            flatten(cache_sums),
            flatten(cache_counts),
            books,
        ),
    )
    grad_query = unflatten(results[0])
    grad_value = unflatten(results[1])
    grad_sums = unflatten(results[2])
    grad_books = unflatten(results[3])
    attended = unflatten(results[4])
    device_grad = jnp.sum(grad_sums, axis=1)
    later_grad = entering(
        device_grad,
        "seq",
        lambda first_part, second_part: first_part + second_part,
        jnp.zeros_like(device_grad),
        True,
    )
    carried = later_grad[:, None] + exclusive_backward(grad_sums)
    picked = jax.vmap(jax.vmap(lambda table_rows, indices: jnp.take(table_rows, indices, axis=0)))(
        carried, code_blocks
    )
    grad_values = (grad_value + picked).astype(jnp.bfloat16)
    book_here = jnp.sum(grad_books, axis=1)
    attended_flat = from_blocks(attended).reshape(tok_here, heads_here * head_width)
    weight_term = inner_rows(attended_flat, full_grad)
    summed_weight, summed_book = lax.psum((weight_term, book_here), "seq")
    grad_weight = summed_weight.astype(jnp.bfloat16)
    return (from_blocks(grad_query), from_blocks(grad_values), summed_book, grad_weight)


F32 = jnp.float32
BF16 = jnp.bfloat16
ANY = pl.BlockSpec(memory_space=pl.ANY)
VMEM = pl.BlockSpec(memory_space=pltpu.VMEM)
SMEM = pl.BlockSpec(memory_space=pltpu.SMEM)
TILE = 256


def dot_nn(a, b):
    return lax.dot_general(a, b, (((1,), (0,)), ((), ())), preferred_element_type=F32)


def dot_nt(a, b):
    return lax.dot_general(a, b, (((1,), (1,)), ((), ())), preferred_element_type=F32)


def slot_block(me, slot, half):
    return jnp.bitwise_xor(me, 2 * slot + half)


def by_head(rows, flip):
    token_major = lax.broadcasted_iota(jnp.int32, (2 * rows, 2 * rows), 1 - flip)
    head_major = lax.broadcasted_iota(jnp.int32, (2 * rows, 2 * rows), flip)
    head = jnp.where(head_major >= rows, 1, 0)
    same = token_major == 2 * (head_major - rows * head) + head
    return jnp.where(same, 1.0, 0.0).astype(BF16)


def causal_tile():
    key_at = lax.broadcasted_iota(jnp.int32, (TILE, TILE), 0)
    query_at = lax.broadcasted_iota(jnp.int32, (TILE, TILE), 1)
    return key_at <= query_at


def pack_kernel(query_ref, value_ref, code_ref, out_ref):
    rows = code_ref.shape[1]
    width = query_ref.shape[1]
    both = jnp.concatenate([query_ref[...], value_ref[...]], axis=1)
    both = dot_nn(by_head(rows, 0), both).astype(BF16)
    for head in range(2):
        for which in range(2):
            column = (2 * which + head) * width
            out_ref[:rows, column : column + width] = both[
                head * rows : (head + 1) * rows, which * width : (which + 1) * width]
        code = code_ref[head : head + 1, :]
        high = lax.shift_right_logical(code, 1)
        for digit, at in ((high, 2 * head), (code - 2 * high, 2 * head + 1)):
            digit = jnp.broadcast_to(digit.astype(F32), (8, rows)).astype(BF16)
            out_ref[rows : rows + 8, at * rows : (at + 1) * rows] = digit


def main_kernel(blocks, heads, width, code_total, me_ref, quarter_ref, *refs):
    slots = refs[:blocks]
    grads = refs[blocks : 5 * blocks]
    book_any, weight_any = refs[5 * blocks : 5 * blocks + 2]
    dq_ref, dv_ref, dbook_any, dweight_any = refs[5 * blocks + 2 : 5 * blocks + 6]
    (q_ref, k_ref, v_ref, k_t_ref, v_t_ref, hot_ref, codes_ref, att_t_ref, lse_ref, weight_ref, go_ref,
     do_t_ref, dk_ref, delta_ref, rows_ref, own_ref, dbook_ref, dweight_ref, book_ref, sems, go_sems, out_sems,
     ) = refs[5 * blocks + 6 :]
    tokens = blocks * BLOCK
    wide = heads * width
    part = grads[0].shape[1]
    me = me_ref[0]
    quarter = quarter_ref[0]

    inputs = [pltpu.make_async_copy(book_any, book_ref, out_sems.at[2 + heads])]
    codes_in, late = [], []
    for at in range(blocks):
        block = slot_block(me, at // 2, at % 2)
        rows = pl.ds(pl.multiple_of(block * BLOCK, BLOCK), BLOCK)
        source = slots[at]
        codes_in.append(pltpu.make_async_copy(
            source.at[pl.ds(BLOCK, 8), :], codes_ref.at[block], sems.at[2, at]))
        inputs.append(pltpu.make_async_copy(
            source.at[pl.ds(0, BLOCK), pl.ds(0, wide)], q_ref.at[rows, :], sems.at[0, at]))
        inputs.append(pltpu.make_async_copy(
            source.at[pl.ds(0, BLOCK), pl.ds(wide, wide)], v_ref.at[rows, :], sems.at[1, at]))
    late.append(pltpu.make_async_copy(weight_any, weight_ref, out_sems.at[0]))
    for at in range(blocks):
        block = slot_block(me, at // 2, at % 2)
        rows = pl.ds(pl.multiple_of(block * BLOCK, BLOCK), BLOCK)
        for piece in range(4):
            column = pl.multiple_of(jnp.bitwise_xor(quarter, piece) * part, part)
            late.append(pltpu.make_async_copy(
                grads[4 * at + piece].at[pl.ds(0, BLOCK), :],
                go_ref.at[rows, pl.ds(column, part)], go_sems.at[at, piece]))
    for copy in codes_in + inputs:
        copy.start()
    for copy in codes_in:
        copy.wait()

    for head in range(heads):
        columns = slice(head * width, (head + 1) * width)
        for block in range(blocks):
            at = head * 2 * BLOCK
            high = codes_ref[block, 0:1, at : at + BLOCK].astype(F32)
            low = codes_ref[block, 0:1, at + BLOCK : at + 2 * BLOCK].astype(F32)
            code = (high * 2.0 + low).astype(jnp.int32)
            rows = lax.broadcasted_iota(jnp.int32, (code_total, BLOCK), 0)
            hot = jnp.where(rows == code, 1.0, 0.0).astype(BF16)
            hot_ref[head, :, block * BLOCK : (block + 1) * BLOCK] = hot
    for copy in inputs:
        copy.wait()
    for copy in late:
        copy.start()
    for head in range(heads):
        columns = slice(head * width, (head + 1) * width)
        key_t = dot_nn(book_ref[head].astype(F32).T.astype(BF16), hot_ref[head])
        k_t_ref[columns, :] = key_t.astype(BF16)
        k_ref[:, columns] = key_t.T.astype(BF16)
        v_t_ref[columns, :] = v_ref[:, columns].astype(F32).T.astype(BF16)

    def scored(head, tile):
        columns = slice(head * width, (head + 1) * width)
        seen = (tile + 1) * TILE
        return dot_nt(k_ref[:seen, columns], q_ref[tile * TILE : seen, columns])

    steps = [(head, tile) for tile in range(tokens // TILE) for head in range(heads)]
    half = len(steps) - tokens // TILE
    ahead = scored(*steps[0])
    for at, (head, tile) in enumerate(steps):
        columns = slice(head * width, (head + 1) * width)
        here = slice(tile * TILE, (tile + 1) * TILE)
        seen = (tile + 1) * TILE
        scores = ahead
        if at + 1 < len(steps):
            ahead = scored(*steps[at + 1])
        if at == half:
            for copy in late:
                copy.wait()
        if at >= half:
            span = slice((at - half) * TILE, (at - half + 1) * TILE)
            do_t_ref[:, span] = dot_nt(weight_ref[...], go_ref[span, :]).astype(BF16)
        last = jnp.where(causal_tile(), scores[seen - TILE :], -jnp.inf)
        scores = last if tile == 0 else jnp.concatenate([scores[: seen - TILE], last], axis=0)
        top = jnp.max(scores, axis=0, keepdims=True)
        weights = jnp.exp(scores - top)
        total = jnp.sum(weights, axis=0, keepdims=True)
        mixed = dot_nn(v_t_ref[columns, :seen], weights.astype(BF16))
        att_t_ref[columns, here] = (mixed / total).astype(BF16)
        lse_ref[head : head + 1, here] = top + jnp.log(total)

    mine = pl.ds(pl.multiple_of(me * BLOCK, BLOCK), BLOCK)
    dq_heads, dv_heads = [], []
    for head in range(heads):
        columns = slice(head * width, (head + 1) * width)
        delta_ref[head : head + 1, :] = jnp.sum(
            do_t_ref[columns, :].astype(F32) * att_t_ref[columns, :].astype(F32), axis=0, keepdims=True)

    def products(head, tile):
        columns = slice(head * width, (head + 1) * width)
        seen = (tile + 1) * TILE
        grad = dot_nn(v_ref[:seen, columns], do_t_ref[columns, tile * TILE : seen])
        return scored(head, tile), grad

    ahead = products(*steps[0])
    for at, (head, tile) in enumerate(steps):
        columns = slice(head * width, (head + 1) * width)
        here = slice(tile * TILE, (tile + 1) * TILE)
        seen = (tile + 1) * TILE
        scores, grad = ahead
        if at + 1 < len(steps):
            ahead = products(*steps[at + 1])
        span = slice(at * TILE, (at + 1) * TILE)
        dweight_ref[:, span] = dot_nn(att_t_ref[...], go_ref[:, span]).astype(BF16)
        weights = jnp.exp(scores - lse_ref[head : head + 1, here])
        last = jnp.where(causal_tile(), weights[seen - TILE :], 0.0)
        weights = last if tile == 0 else jnp.concatenate([weights[: seen - TILE], last], axis=0)
        grad = (weights * (grad - delta_ref[head : head + 1, here])).astype(BF16)
        term = dot_nn(grad, q_ref[here, columns])
        if tile == 0:
            dk_ref[head, :seen, :] = term
        else:
            dk_ref[head, : seen - TILE, :] += term[: seen - TILE]
            dk_ref[head, seen - TILE : seen, :] = term[seen - TILE :]
    outputs = [pltpu.make_async_copy(dweight_ref, dweight_any, out_sems.at[1])]
    outputs[0].start()
    for head in range(heads):
        columns = slice(head * width, (head + 1) * width)
        dbook_ref[head] = dot_nn(hot_ref[head], dk_ref[head].astype(BF16))
        outputs.append(pltpu.make_async_copy(dbook_ref.at[head], dbook_any.at[head], out_sems.at[2 + head]))
        outputs[-1].start()
    early_key = lax.broadcasted_iota(jnp.int32, (BLOCK, tokens), 0) + me * BLOCK
    later_query = lax.broadcasted_iota(jnp.int32, (BLOCK, tokens), 1)
    any_key = lax.broadcasted_iota(jnp.int32, (tokens, BLOCK), 0)
    own_query = lax.broadcasted_iota(jnp.int32, (tokens, BLOCK), 1) + me * BLOCK
    staged = []
    for head in range(heads):
        columns = slice(head * width, (head + 1) * width)
        for block in range(blocks):
            span = slice(block * BLOCK, (block + 1) * BLOCK)
            rows_ref[2 * head, block : block + 1, :] = lse_ref[head : head + 1, span]
            rows_ref[2 * head + 1, block : block + 1, :] = delta_ref[head : head + 1, span]
            own_ref[head, block] = do_t_ref[columns, span]
        staged.append((
            dot_nt(k_ref[mine, columns], q_ref[:, columns]),
            dot_nt(k_ref[:, columns], q_ref[mine, columns]),
            dot_nn(v_ref[:, columns], own_ref[head, me]),
        ))
    for head, (key_scores, query_scores, grad) in enumerate(staged):
        columns = slice(head * width, (head + 1) * width)
        weights = jnp.exp(jnp.where(
            early_key <= later_query, key_scores - lse_ref[head : head + 1, :], -jnp.inf))
        dv_heads.append(dot_nt(weights.astype(BF16), do_t_ref[columns, :]).astype(BF16))
        own_lse = rows_ref[2 * head, pl.ds(me, 1), :]
        own_delta = rows_ref[2 * head + 1, pl.ds(me, 1), :]
        weights = jnp.exp(jnp.where(any_key <= own_query, query_scores - own_lse, -jnp.inf))
        grad = (weights * (grad - own_delta)).astype(BF16)
        dq_heads.append(dot_nn(k_t_ref[columns, :], grad).T.astype(BF16))
    mix = by_head(BLOCK, 1)
    dq_ref[...] = dot_nn(mix, jnp.concatenate(dq_heads, axis=0)).astype(BF16)
    dv_ref[...] = dot_nn(mix, jnp.concatenate(dv_heads, axis=0)).astype(BF16)
    for copy in outputs:
        copy.wait()


def gathered_on_device(*arrays):
    return gathered_body(*arrays)


def gathered_body(queries, values, codes, codebook, out_weight, grad_out):
    blocks = lax.axis_size("seq")
    tok_here, heads, width = queries.shape
    code_total = codebook.shape[1]
    wide = heads * width
    part = grad_out.shape[1]
    if tok_here != BLOCK or part != 2 * wide or 2 * wide != 4 * BLOCK:
        raise ValueError("unexpected shapes")
    tokens = blocks * BLOCK
    me = lax.axis_index("seq").astype(jnp.int32).reshape(1)
    quarter = lax.axis_index("head").astype(jnp.int32).reshape(1)

    payload = pl.pallas_call(
        pack_kernel,
        out_shape=jax.ShapeDtypeStruct((BLOCK + 8, part), BF16),
        in_specs=[VMEM] * 3,
        out_specs=VMEM,
        compiler_params=pltpu.CompilerParams(vmem_limit_bytes=4 * 2**20),
        name="pack",
    )(*(
        pltpu.with_memory_space_constraint(array, pltpu.HBM)
        for array in (queries.reshape(heads * BLOCK, width), values.reshape(heads * BLOCK, width), codes)
    ))

    def exchange(array, axis, flip):
        pairs = [(i, i ^ flip) for i in range(lax.axis_size(axis))]
        return lax.ppermute(array, axis, pairs)

    def along_seq(array):
        near = exchange(array, "seq", 2)
        far = exchange(array, "seq", 4)
        held = []
        for block in (array, near, far, exchange(far, "seq", 2)):
            held += [block, exchange(block, "seq", 1)]
        return held

    slots = along_seq(payload)
    grads = []
    for own in along_seq(grad_out):
        across = exchange(own, "head", 2)
        grads += [own, exchange(own, "head", 1), across, exchange(across, "head", 1)]

    main = pl.pallas_call(
        functools.partial(main_kernel, blocks, heads, width, code_total),
        out_shape=(
            jax.ShapeDtypeStruct((heads * BLOCK, width), BF16),
            jax.ShapeDtypeStruct((heads * BLOCK, width), BF16),
            jax.ShapeDtypeStruct((heads, code_total, width), F32),
            jax.ShapeDtypeStruct((wide, 4 * part), BF16),
        ),
        in_specs=[SMEM, SMEM] + [ANY] * (5 * blocks + 2),
        out_specs=(VMEM, VMEM, ANY, ANY),
        scratch_shapes=[
            pltpu.VMEM((tokens, wide), BF16),
            pltpu.VMEM((tokens, wide), BF16),
            pltpu.VMEM((tokens, wide), BF16),
            pltpu.VMEM((wide, tokens), BF16),
            pltpu.VMEM((wide, tokens), BF16),
            pltpu.VMEM((heads, code_total, tokens), BF16),
            pltpu.VMEM((blocks, 8, 4 * BLOCK), BF16),
            pltpu.VMEM((wide, tokens), BF16),
            pltpu.VMEM((8, tokens), F32),
            pltpu.VMEM((wide, 4 * part), BF16),
            pltpu.VMEM((tokens, 4 * part), BF16),
            pltpu.VMEM((wide, tokens), BF16),
            pltpu.VMEM((heads, tokens, width), F32),
            pltpu.VMEM((8, tokens), F32),
            pltpu.VMEM((2 * heads, blocks, BLOCK), F32),
            pltpu.VMEM((heads, blocks, width, BLOCK), BF16),
            pltpu.VMEM((heads, code_total, width), F32),
            pltpu.VMEM((wide, 4 * part), BF16),
            pltpu.VMEM((heads, code_total, width), BF16),
            pltpu.SemaphoreType.DMA((3, blocks)),
            pltpu.SemaphoreType.DMA((blocks, 4)),
            pltpu.SemaphoreType.DMA((3 + heads,)),
        ],
        compiler_params=pltpu.CompilerParams(vmem_limit_bytes=28 * 2**20),
        cost_estimate=pl.CostEstimate(flops=5 * 10**9, bytes_accessed=8 * 10**6, transcendentals=10**6),
        name="main",
    )
    grads[0], codebook, out_weight = (
        pltpu.with_memory_space_constraint(array, pltpu.HBM)
        for array in (grads[0], codebook, out_weight)
    )
    dq, dv, dbook, dweight = main(me, quarter, *slots, *grads, codebook, out_weight)
    shape = (tok_here, heads, width)
    return (dq.reshape(shape), dv.reshape(shape), dbook, dweight)


def solution(mesh):
    body = on_device
    gathered = mesh.shape["seq"] == 8 and mesh.shape["head"] == 4
    if gathered:
        body = gathered_on_device
    return jax.shard_map(
        body,
        mesh=mesh,
        in_specs=(
            P("seq", "head", None),
            P("seq", "head", None),
            P("head", "seq"),
            P("head", None, None),
            P("head", None),
            P("seq", "head"),
        ),
        out_specs=(
            P("seq", "head", None),
            P("seq", "head", None),
            P("head", None, None),
            P("head", None),
        ),
        check_vma=False,
    )
```

```python
import functools

import jax
import jax.numpy as jnp
from jax import lax
from jax.experimental import pallas as pl
from jax.experimental.pallas import tpu as pltpu
from jax.sharding import PartitionSpec as P


BLOCK = 128


def entering(value, axis, join, neutral, backward):
    count, mine = (lax.axis_size(axis), lax.axis_index(axis))
    pieces = jax.tree.map(lambda part: lax.all_gather(part, axis), value)
    if backward:
        pieces = jax.tree.map(lambda part: part[::-1], pieces)
        mine = count - 1 - mine
    so_far = jax.tree.map(
        lambda part, zero: jnp.full_like(part, 0) + jnp.asarray(zero, part.dtype), value, neutral
    )

    def turn(position, so_far):
        longer = join(so_far, jax.tree.map(lambda part: part[position], pieces))
        return jax.tree.map(lambda new, old: jnp.where(position < mine, new, old), longer, so_far)

    return lax.fori_loop(0, count - 1, turn, so_far)


def inner_rows(left_side, right_side):
    return lax.dot_general(
        left_side, right_side, (((0,), (0,)), ((), ())), preferred_element_type=jnp.float32
    )


def block_core(query_rows, code_rows, value_rows, grad_rows, cache_sum, cache_count, codebook_head):
    key_rows = jnp.take(codebook_head, code_rows, axis=0)
    contract_last = (((1,), (1,)), ((), ()))
    local_score = lax.dot_general(
        query_rows, key_rows, contract_last, preferred_element_type=jnp.float32
    )
    code_score = lax.dot_general(
        query_rows, codebook_head, contract_last, preferred_element_type=jnp.float32
    )
    length = query_rows.shape[0]
    row_index = lax.broadcasted_iota(jnp.int32, (length, length), 0)
    col_index = lax.broadcasted_iota(jnp.int32, (length, length), 1)
    causal = col_index <= row_index
    top_score = jnp.maximum(
        jnp.max(jnp.where(causal, local_score, -jnp.inf), axis=1), jnp.max(code_score, axis=1)
    )
    weights = jnp.where(causal, jnp.exp(local_score - top_score[:, None]), jnp.float32(0.0))
    cache_weight = jnp.exp(code_score - top_score[:, None])
    denominator = jnp.sum(weights, axis=1) + jnp.sum(cache_weight * cache_count[None, :], axis=1)
    cache_round = cache_sum.astype(jnp.bfloat16)
    numerator = jnp.dot(
        weights.astype(jnp.bfloat16), value_rows, preferred_element_type=jnp.float32
    )
    numerator = numerator + jnp.dot(
        cache_weight.astype(jnp.bfloat16), cache_round, preferred_element_type=jnp.float32
    )
    attended = numerator / denominator[:, None]
    row_delta = jnp.sum(grad_rows.astype(jnp.float32) * attended, axis=1)
    local_grad = lax.dot_general(
        grad_rows, value_rows, contract_last, preferred_element_type=jnp.float32
    )
    cache_grad = lax.dot_general(
        grad_rows, cache_round, contract_last, preferred_element_type=jnp.float32
    )
    grad_local = (weights * (local_grad - row_delta[:, None]) / denominator[:, None]).astype(
        jnp.bfloat16
    )
    grad_cache = (
        cache_weight
        * (cache_grad - row_delta[:, None] * cache_count[None, :])
        / denominator[:, None]
    ).astype(jnp.bfloat16)
    grad_query = jnp.dot(grad_local, key_rows, preferred_element_type=jnp.float32)
    grad_query = (
        grad_query + jnp.dot(grad_cache, codebook_head, preferred_element_type=jnp.float32)
    ).astype(jnp.bfloat16)
    grad_key = inner_rows(grad_local, query_rows)
    key_high = grad_key.astype(jnp.bfloat16)
    key_low = (grad_key - key_high.astype(jnp.float32)).astype(jnp.bfloat16)
    selector = (
        code_rows[:, None] == jnp.arange(codebook_head.shape[0], dtype=jnp.int32)[None, :]
    ).astype(jnp.bfloat16)
    grad_book = inner_rows(selector, key_high) + inner_rows(selector, key_low)
    grad_book = grad_book + inner_rows(grad_cache, query_rows)
    local_share = (weights / denominator[:, None]).astype(jnp.bfloat16)
    cache_share = (cache_weight / denominator[:, None]).astype(jnp.bfloat16)
    grad_value = inner_rows(local_share, grad_rows)
    grad_sum = inner_rows(cache_share, grad_rows)
    return (grad_query, grad_value, grad_sum, grad_book, attended.astype(jnp.bfloat16))


def exclusive_forward(stacked):
    summed = jnp.cumsum(stacked, axis=1)
    return jnp.concatenate([jnp.zeros_like(stacked), summed[:, :-1]], axis=1)


def exclusive_backward(stacked):
    summed = jnp.flip(jnp.cumsum(jnp.flip(stacked, axis=1), axis=1), axis=1)
    return jnp.concatenate([summed[:, 1:], jnp.zeros_like(stacked)], axis=1)


def on_device(queries, values, codes, codebook, out_weight, grad_out):
    tok_here, heads_here, head_width = queries.shape
    code_total = codebook.shape[1]
    blocks = tok_here // BLOCK
    full_grad = lax.all_gather(grad_out, "head", axis=1, tiled=True)
    grad_flat = lax.dot_general(
        full_grad, out_weight, (((1,), (1,)), ((), ())), preferred_element_type=jnp.float32
    ).astype(jnp.bfloat16)
    grad_heads = grad_flat.reshape(tok_here, heads_here, head_width)

    def to_blocks(array):
        return jnp.moveaxis(array.reshape(blocks, BLOCK, heads_here, head_width), 2, 0)

    def from_blocks(array):
        return jnp.moveaxis(array, 0, 2).reshape(tok_here, heads_here, head_width)

    def flatten(array):
        return array.reshape((heads_here * blocks,) + array.shape[2:])

    def unflatten(array):
        return array.reshape((heads_here, blocks) + array.shape[1:])

    code_blocks = codes.reshape(heads_here, blocks, BLOCK)
    query_blocks = to_blocks(queries)
    value_blocks = to_blocks(values)
    grad_blocks = to_blocks(grad_heads)
    selector = (code_blocks[..., None] == jnp.arange(code_total, dtype=jnp.int32)).astype(
        jnp.bfloat16
    )
    block_sums = jnp.einsum(
        "hnbc,hnbd->hncd", selector, value_blocks, preferred_element_type=jnp.float32
    )
    block_counts = jnp.sum(selector, axis=2, dtype=jnp.float32)
    device_parts = (jnp.sum(block_sums, axis=1), jnp.sum(block_counts, axis=1))
    earlier = entering(
        device_parts,
        "seq",
        lambda first_part, second_part: (
            first_part[0] + second_part[0],
            first_part[1] + second_part[1],
        ),
        (jnp.zeros_like(device_parts[0]), jnp.zeros_like(device_parts[1])),
        False,
    )
    cache_sums = earlier[0][:, None] + exclusive_forward(block_sums)
    cache_counts = earlier[1][:, None] + exclusive_forward(block_counts)
    books = jnp.repeat(codebook, blocks, axis=0)
    results = lax.map(
        lambda block_items: block_core(*block_items),
        (
            flatten(query_blocks),
            flatten(code_blocks),
            flatten(value_blocks),
            flatten(grad_blocks),
            flatten(cache_sums),
            flatten(cache_counts),
            books,
        ),
    )
    grad_query = unflatten(results[0])
    grad_value = unflatten(results[1])
    grad_sums = unflatten(results[2])
    grad_books = unflatten(results[3])
    attended = unflatten(results[4])
    device_grad = jnp.sum(grad_sums, axis=1)
    later_grad = entering(
        device_grad,
        "seq",
        lambda first_part, second_part: first_part + second_part,
        jnp.zeros_like(device_grad),
        True,
    )
    carried = later_grad[:, None] + exclusive_backward(grad_sums)
    picked = jax.vmap(jax.vmap(lambda table_rows, indices: jnp.take(table_rows, indices, axis=0)))(
        carried, code_blocks
    )
    grad_values = (grad_value + picked).astype(jnp.bfloat16)
    book_here = jnp.sum(grad_books, axis=1)
    attended_flat = from_blocks(attended).reshape(tok_here, heads_here * head_width)
    weight_term = inner_rows(attended_flat, full_grad)
    summed_weight, summed_book = lax.psum((weight_term, book_here), "seq")
    grad_weight = summed_weight.astype(jnp.bfloat16)
    return (from_blocks(grad_query), from_blocks(grad_values), summed_book, grad_weight)


F32 = jnp.float32
BF16 = jnp.bfloat16
ANY = pl.BlockSpec(memory_space=pl.ANY)
VMEM = pl.BlockSpec(memory_space=pltpu.VMEM)
SMEM = pl.BlockSpec(memory_space=pltpu.SMEM)
TILE = 256


def dot_nn(a, b):
    return lax.dot_general(a, b, (((1,), (0,)), ((), ())), preferred_element_type=F32)


def dot_nt(a, b):
    return lax.dot_general(a, b, (((1,), (1,)), ((), ())), preferred_element_type=F32)


def slot_block(me, slot, half):
    return jnp.bitwise_xor(me, 2 * slot + half)


def by_head(rows, flip):
    token_major = lax.broadcasted_iota(jnp.int32, (2 * rows, 2 * rows), 1 - flip)
    head_major = lax.broadcasted_iota(jnp.int32, (2 * rows, 2 * rows), flip)
    head = jnp.where(head_major >= rows, 1, 0)
    same = token_major == 2 * (head_major - rows * head) + head
    return jnp.where(same, 1.0, 0.0).astype(BF16)


def causal_tile():
    key_at = lax.broadcasted_iota(jnp.int32, (TILE, TILE), 0)
    query_at = lax.broadcasted_iota(jnp.int32, (TILE, TILE), 1)
    return key_at <= query_at


def pack_kernel(query_ref, value_ref, code_ref, out_ref):
    rows = code_ref.shape[1]
    width = query_ref.shape[1]
    both = jnp.concatenate([query_ref[...], value_ref[...]], axis=1)
    both = dot_nn(by_head(rows, 0), both).astype(BF16)
    for head in range(2):
        for which in range(2):
            column = (2 * which + head) * width
            out_ref[:rows, column : column + width] = both[
                head * rows : (head + 1) * rows, which * width : (which + 1) * width]
        code = code_ref[head : head + 1, :]
        high = lax.shift_right_logical(code, 1)
        for digit, at in ((high, 2 * head), (code - 2 * high, 2 * head + 1)):
            digit = jnp.broadcast_to(digit.astype(F32), (8, rows)).astype(BF16)
            out_ref[rows : rows + 8, at * rows : (at + 1) * rows] = digit


def main_kernel(blocks, heads, width, code_total, me_ref, quarter_ref, *refs):
    slots = refs[:blocks]
    grads = refs[blocks : 5 * blocks]
    book_any, weight_any = refs[5 * blocks : 5 * blocks + 2]
    dq_ref, dv_ref, dbook_any, dweight_any = refs[5 * blocks + 2 : 5 * blocks + 6]
    (q_ref, k_ref, v_ref, k_t_ref, v_t_ref, hot_ref, codes_ref, att_t_ref, lse_ref, weight_ref, go_ref,
     do_t_ref, dk_ref, delta_ref, rows_ref, own_ref, dbook_ref, dweight_ref, book_ref, kept_ref, sems, go_sems, out_sems,
     ) = refs[5 * blocks + 6 :]
    tokens = blocks * BLOCK
    wide = heads * width
    part = grads[0].shape[1]
    me = me_ref[0]
    quarter = quarter_ref[0]

    inputs = [pltpu.make_async_copy(book_any, book_ref, out_sems.at[2 + heads])]
    codes_in, late = [], []
    for at in range(blocks):
        block = slot_block(me, at // 2, at % 2)
        rows = pl.ds(pl.multiple_of(block * BLOCK, BLOCK), BLOCK)
        source = slots[at]
        codes_in.append(pltpu.make_async_copy(
            source.at[pl.ds(BLOCK, 8), :], codes_ref.at[block], sems.at[2, at]))
        inputs.append(pltpu.make_async_copy(
            source.at[pl.ds(0, BLOCK), pl.ds(0, wide)], q_ref.at[rows, :], sems.at[0, at]))
        inputs.append(pltpu.make_async_copy(
            source.at[pl.ds(0, BLOCK), pl.ds(wide, wide)], v_ref.at[rows, :], sems.at[1, at]))
    late.append(pltpu.make_async_copy(weight_any, weight_ref, out_sems.at[0]))
    for at in range(blocks):
        block = slot_block(me, at // 2, at % 2)
        rows = pl.ds(pl.multiple_of(block * BLOCK, BLOCK), BLOCK)
        for piece in range(4):
            column = pl.multiple_of(jnp.bitwise_xor(quarter, piece) * part, part)
            late.append(pltpu.make_async_copy(
                grads[4 * at + piece].at[pl.ds(0, BLOCK), :],
                go_ref.at[rows, pl.ds(column, part)], go_sems.at[at, piece]))
    for copy in codes_in + inputs:
        copy.start()
    for copy in codes_in:
        copy.wait()

    for head in range(heads):
        columns = slice(head * width, (head + 1) * width)
        for block in range(blocks):
            at = head * 2 * BLOCK
            high = codes_ref[block, 0:1, at : at + BLOCK].astype(F32)
            low = codes_ref[block, 0:1, at + BLOCK : at + 2 * BLOCK].astype(F32)
            code = (high * 2.0 + low).astype(jnp.int32)
            rows = lax.broadcasted_iota(jnp.int32, (code_total, BLOCK), 0)
            hot = jnp.where(rows == code, 1.0, 0.0).astype(BF16)
            hot_ref[head, :, block * BLOCK : (block + 1) * BLOCK] = hot
    for copy in inputs:
        copy.wait()
    for copy in late:
        copy.start()
    for head in range(heads):
        columns = slice(head * width, (head + 1) * width)
        key_t = dot_nn(book_ref[head].astype(F32).T.astype(BF16), hot_ref[head])
        k_t_ref[columns, :] = key_t.astype(BF16)
        k_ref[:, columns] = key_t.T.astype(BF16)
        v_t_ref[columns, :] = v_ref[:, columns].astype(F32).T.astype(BF16)

    def scored(head, tile):
        columns = slice(head * width, (head + 1) * width)
        seen = (tile + 1) * TILE
        return dot_nt(k_ref[:seen, columns], q_ref[tile * TILE : seen, columns])

    steps = [(head, tile) for tile in range(tokens // TILE) for head in range(heads)]
    half = len(steps) - tokens // TILE
    ahead = scored(*steps[0])
    for at, (head, tile) in enumerate(steps):
        columns = slice(head * width, (head + 1) * width)
        here = slice(tile * TILE, (tile + 1) * TILE)
        seen = (tile + 1) * TILE
        scores = ahead
        if at + 1 < len(steps):
            ahead = scored(*steps[at + 1])
        if at == half:
            for copy in late:
                copy.wait()
        if at >= half:
            span = slice((at - half) * TILE, (at - half + 1) * TILE)
            do_t_ref[:, span] = dot_nt(weight_ref[...], go_ref[span, :]).astype(BF16)
        last = jnp.where(causal_tile(), scores[seen - TILE :], -jnp.inf)
        scores = last if tile == 0 else jnp.concatenate([scores[: seen - TILE], last], axis=0)
        top = jnp.max(scores, axis=0, keepdims=True)
        weights = jnp.exp(scores - top)
        total = jnp.sum(weights, axis=0, keepdims=True)
        weights = weights.astype(BF16)
        kept_ref[head, :seen, here] = weights
        mixed = dot_nn(v_t_ref[columns, :seen], weights)
        share = 1.0 / total
        att_t_ref[columns, here] = (mixed * share).astype(BF16)
        lse_ref[heads + head : heads + head + 1, here] = share
        lse_ref[head : head + 1, here] = top + jnp.log(total)

    mine = pl.ds(pl.multiple_of(me * BLOCK, BLOCK), BLOCK)
    dq_heads, dv_heads = [], []
    for head in range(heads):
        columns = slice(head * width, (head + 1) * width)
        delta_ref[head : head + 1, :] = jnp.sum(
            do_t_ref[columns, :].astype(F32) * att_t_ref[columns, :].astype(F32), axis=0, keepdims=True)

    def products(head, tile):
        columns = slice(head * width, (head + 1) * width)
        seen = (tile + 1) * TILE
        grad = dot_nn(v_ref[:seen, columns], do_t_ref[columns, tile * TILE : seen])
        return grad

    ahead = products(*steps[0])
    for at, (head, tile) in enumerate(steps):
        columns = slice(head * width, (head + 1) * width)
        here = slice(tile * TILE, (tile + 1) * TILE)
        seen = (tile + 1) * TILE
        grad = ahead
        if at + 1 < len(steps):
            ahead = products(*steps[at + 1])
        span = slice(at * TILE, (at + 1) * TILE)
        dweight_ref[:, span] = dot_nn(att_t_ref[...], go_ref[:, span]).astype(BF16)
        grad = (grad - delta_ref[head : head + 1, here]) * lse_ref[heads + head : heads + head + 1, here]
        grad = (kept_ref[head, :seen, here].astype(F32) * grad).astype(BF16)
        term = dot_nn(grad, q_ref[here, columns])
        if tile == 0:
            dk_ref[head, :seen, :] = term
        else:
            dk_ref[head, : seen - TILE, :] += term[: seen - TILE]
            dk_ref[head, seen - TILE : seen, :] = term[seen - TILE :]
    outputs = [pltpu.make_async_copy(dweight_ref, dweight_any, out_sems.at[1])]
    outputs[0].start()
    for head in range(heads):
        columns = slice(head * width, (head + 1) * width)
        dbook_ref[head] = dot_nn(hot_ref[head], dk_ref[head].astype(BF16))
        outputs.append(pltpu.make_async_copy(dbook_ref.at[head], dbook_any.at[head], out_sems.at[2 + head]))
        outputs[-1].start()
    early_key = lax.broadcasted_iota(jnp.int32, (BLOCK, tokens), 0) + me * BLOCK
    later_query = lax.broadcasted_iota(jnp.int32, (BLOCK, tokens), 1)
    any_key = lax.broadcasted_iota(jnp.int32, (tokens, BLOCK), 0)
    own_query = lax.broadcasted_iota(jnp.int32, (tokens, BLOCK), 1) + me * BLOCK
    staged = []
    for head in range(heads):
        columns = slice(head * width, (head + 1) * width)
        for block in range(blocks):
            span = slice(block * BLOCK, (block + 1) * BLOCK)
            rows_ref[2 * head, block : block + 1, :] = lse_ref[head : head + 1, span]
            rows_ref[2 * head + 1, block : block + 1, :] = delta_ref[head : head + 1, span]
            own_ref[head, block] = do_t_ref[columns, span]
        staged.append((
            dot_nt(k_ref[mine, columns], q_ref[:, columns]),
            dot_nt(k_ref[:, columns], q_ref[mine, columns]),
            dot_nn(v_ref[:, columns], own_ref[head, me]),
        ))
    for head, (key_scores, query_scores, grad) in enumerate(staged):
        columns = slice(head * width, (head + 1) * width)
        weights = jnp.exp(jnp.where(
            early_key <= later_query, key_scores - lse_ref[head : head + 1, :], -jnp.inf))
        dv_heads.append(dot_nt(weights.astype(BF16), do_t_ref[columns, :]).astype(BF16))
        own_lse = rows_ref[2 * head, pl.ds(me, 1), :]
        own_delta = rows_ref[2 * head + 1, pl.ds(me, 1), :]
        weights = jnp.exp(jnp.where(any_key <= own_query, query_scores - own_lse, -jnp.inf))
        grad = (weights * (grad - own_delta)).astype(BF16)
        dq_heads.append(dot_nn(k_t_ref[columns, :], grad).T.astype(BF16))
    mix = by_head(BLOCK, 1)
    dq_ref[...] = dot_nn(mix, jnp.concatenate(dq_heads, axis=0)).astype(BF16)
    dv_ref[...] = dot_nn(mix, jnp.concatenate(dv_heads, axis=0)).astype(BF16)
    for copy in outputs:
        copy.wait()


def gathered_on_device(*arrays):
    return gathered_body(*arrays)


def gathered_body(queries, values, codes, codebook, out_weight, grad_out):
    blocks = lax.axis_size("seq")
    tok_here, heads, width = queries.shape
    code_total = codebook.shape[1]
    wide = heads * width
    part = grad_out.shape[1]
    if tok_here != BLOCK or part != 2 * wide or 2 * wide != 4 * BLOCK:
        raise ValueError("unexpected shapes")
    tokens = blocks * BLOCK
    me = lax.axis_index("seq").astype(jnp.int32).reshape(1)
    quarter = lax.axis_index("head").astype(jnp.int32).reshape(1)

    payload = pl.pallas_call(
        pack_kernel,
        out_shape=jax.ShapeDtypeStruct((BLOCK + 8, part), BF16),
        in_specs=[VMEM] * 3,
        out_specs=VMEM,
        compiler_params=pltpu.CompilerParams(vmem_limit_bytes=4 * 2**20),
        name="pack",
    )(*(
        pltpu.with_memory_space_constraint(array, pltpu.HBM)
        for array in (queries.reshape(heads * BLOCK, width), values.reshape(heads * BLOCK, width), codes)
    ))

    def exchange(array, axis, flip):
        pairs = [(i, i ^ flip) for i in range(lax.axis_size(axis))]
        return lax.ppermute(array, axis, pairs)

    def along_seq(array):
        near = exchange(array, "seq", 2)
        far = exchange(array, "seq", 4)
        held = []
        for block in (array, near, far, exchange(far, "seq", 2)):
            held += [block, exchange(block, "seq", 1)]
        return held

    slots = along_seq(payload)
    grads = []
    for own in along_seq(grad_out):
        across = exchange(own, "head", 2)
        grads += [own, exchange(own, "head", 1), across, exchange(across, "head", 1)]

    main = pl.pallas_call(
        functools.partial(main_kernel, blocks, heads, width, code_total),
        out_shape=(
            jax.ShapeDtypeStruct((heads * BLOCK, width), BF16),
            jax.ShapeDtypeStruct((heads * BLOCK, width), BF16),
            jax.ShapeDtypeStruct((heads, code_total, width), F32),
            jax.ShapeDtypeStruct((wide, 4 * part), BF16),
        ),
        in_specs=[SMEM, SMEM] + [ANY] * (5 * blocks + 2),
        out_specs=(VMEM, VMEM, ANY, ANY),
        scratch_shapes=[
            pltpu.VMEM((tokens, wide), BF16),
            pltpu.VMEM((tokens, wide), BF16),
            pltpu.VMEM((tokens, wide), BF16),
            pltpu.VMEM((wide, tokens), BF16),
            pltpu.VMEM((wide, tokens), BF16),
            pltpu.VMEM((heads, code_total, tokens), BF16),
            pltpu.VMEM((blocks, 8, 4 * BLOCK), BF16),
            pltpu.VMEM((wide, tokens), BF16),
            pltpu.VMEM((8, tokens), F32),
            pltpu.VMEM((wide, 4 * part), BF16),
            pltpu.VMEM((tokens, 4 * part), BF16),
            pltpu.VMEM((wide, tokens), BF16),
            pltpu.VMEM((heads, tokens, width), F32),
            pltpu.VMEM((8, tokens), F32),
            pltpu.VMEM((2 * heads, blocks, BLOCK), F32),
            pltpu.VMEM((heads, blocks, width, BLOCK), BF16),
            pltpu.VMEM((heads, code_total, width), F32),
            pltpu.VMEM((wide, 4 * part), BF16),
            pltpu.VMEM((heads, code_total, width), BF16),
            pltpu.VMEM((heads, tokens, tokens), BF16),
            pltpu.SemaphoreType.DMA((3, blocks)),
            pltpu.SemaphoreType.DMA((blocks, 4)),
            pltpu.SemaphoreType.DMA((3 + heads,)),
        ],
        compiler_params=pltpu.CompilerParams(vmem_limit_bytes=32 * 2**20),
        cost_estimate=pl.CostEstimate(flops=5 * 10**9, bytes_accessed=8 * 10**6, transcendentals=10**6),
        name="main",
    )
    grads[0], codebook, out_weight = (
        pltpu.with_memory_space_constraint(array, pltpu.HBM)
        for array in (grads[0], codebook, out_weight)
    )
    dq, dv, dbook, dweight = main(me, quarter, *slots, *grads, codebook, out_weight)
    shape = (tok_here, heads, width)
    return (dq.reshape(shape), dv.reshape(shape), dbook, dweight)


def solution(mesh):
    body = on_device
    gathered = mesh.shape["seq"] == 8 and mesh.shape["head"] == 4
    if gathered:
        body = gathered_on_device
    return jax.shard_map(
        body,
        mesh=mesh,
        in_specs=(
            P("seq", "head", None),
            P("seq", "head", None),
            P("head", "seq"),
            P("head", None, None),
            P("head", None),
            P("seq", "head"),
        ),
        out_specs=(
            P("seq", "head", None),
            P("seq", "head", None),
            P("head", None, None),
            P("head", None),
        ),
        check_vma=False,
    )
```
